256 devices in a mesh: img: 8 (over x, y_lo), atom: 32 (over y_hi, z, core).
Axes of the slice: x: 4, y: 4 (y_hi: 2, y_lo: 2; y = y_hi * 2 + y_lo), z: 8, core: 2. Of those that a mesh axis runs over, the one named last changes fastest.
Arguments:
- positions: float32 [8, 3, 32768], P('img', None, 'atom'), may hold values from -14.6 to 14.6, as said below
- species: int32 [32768], P('atom'), may hold values from 0 to 3
- counts: int32 [32768], P('atom'), may hold values from 1 to 16, as said below
- neighbours: int32 [16, 32768], P(None, 'atom'), may hold values from 0 to 1535, as said below
- send_list: int32 [16384], P('atom'), may hold values from 0 to 1023
- climb: int32 [8], P('img'), may hold values 0 or 1
- embed: bfloat16 [4, 128], replicated, may hold values from -6 to 6
- ref_energy: float32 [4], replicated, may hold values from -2 to 2
- rad_in: bfloat16 [3, 8, 64], replicated, may hold values from -24 to 24
- rad_out: bfloat16 [3, 64, 128], replicated, may hold values from -0.047851562 to 0.047851562
- mixing: bfloat16 [2, 128, 128], replicated, may hold values from -0.5 to 0.5
- w_energy: bfloat16 [128], replicated, may hold values from -0.5 to 0.5
Outputs:
- neb_force: float32 [8, 3, 32768], P('img', None, 'atom')
- energies: float32 [8], P('img')
The draws below stay inside these ranges and needn't reach their ends.
Inputs may be any that keep to these rules, and one draw needn't show every extreme that they name: `positions`: positions of image p are those of image 0 plus a sum of p random displacements. `counts`: the first atom of every tile has all 16 slots live. `neighbours`: every slot of the atom with local index i (its index mod 1024) names a row from i to i + 512 of its tile's table, never row i + 256. `send_list`: values are local atom indices of the owning tile.
All inputs are finite; a program needn't handle non-finite values. No bound on the sum of `climb` on one device may be relied on, other than what follows from the above.
Results may differ from the reference program's by a relative error of at most 0.007.
Values may be sent and summed in bfloat16 or wider, within the bound.
A program may use at most 64 MiB of HBM per device.

```python
import math
import jax
import jax.numpy as jnp
from jax import lax

C = 128
RAD = 64
NB = 8
SPECIES = 4
LAYERS = 2
NBR = 16
HALO = 256
ATOM_DEV = 1024
ATOMS = 32768
IMAGES = 8
N_ATOM = 32


def draw_positions(key, part):
    first, second, third, fourth, fifth, sixth = jax.random.split(key, 6)
    base = jnp.clip(jax.random.normal(first, (3, ATOMS), jnp.float32), -5.0, 5.0)
    tile_total = ATOMS // ATOM_DEV
    tile_of = jnp.arange(ATOMS, dtype=jnp.int32) // ATOM_DEV
    hot_tiles = jax.random.randint(fourth, (2,), 0, tile_total)
    cold_weight = jnp.exp(jax.random.uniform(fifth, (tile_total,), jnp.float32, jnp.log(0.003), jnp.log(0.1)))
    atom_weight = jnp.take(cold_weight, tile_of)
    is_hot = jnp.logical_or(tile_of == hot_tiles[0], tile_of == hot_tiles[1])
    atom_weight = jnp.where(is_hot, 1.0, atom_weight)
    path_dir = jnp.clip(jax.random.normal(second, (3, ATOMS), jnp.float32), -2.5, 2.5)
    wobble = jnp.clip(jax.random.normal(sixth, (IMAGES, 3, ATOMS), jnp.float32), -2.5, 2.5)
    moves = (path_dir[None] + 0.5 * wobble) * atom_weight[None, None, :]
    scales = jnp.exp(jax.random.uniform(third, (IMAGES, 1, 1), jnp.float32, jnp.log(0.05), jnp.log(0.3)))
    order = jax.lax.broadcasted_iota(jnp.int32, (IMAGES, 1, 1), 0)
    moves = jnp.where(order == 0, 0.0, moves * scales)
    return base[None] + jnp.cumsum(moves, axis=0)


def draw_counts(key, part):
    raw = jax.random.randint(key, (ATOMS,), 1, NBR + 1)
    first = jnp.arange(ATOMS, dtype=jnp.int32) % ATOM_DEV == 0
    return jnp.where(first, NBR, raw).astype(jnp.int32)


def draw_neighbours(key, part):
    raw = jax.random.randint(key, (NBR, ATOMS), -HALO, HALO)
    offset = jnp.where(raw >= 0, raw + 1, raw)
    local = (jnp.arange(ATOMS, dtype=jnp.int32) % ATOM_DEV)[None, :]
    slot = jax.lax.broadcasted_iota(jnp.int32, (NBR, ATOMS), 0)
    offset = jnp.where(jnp.logical_and(slot == 0, local == 0), -HALO, offset)
    offset = jnp.where(jnp.logical_and(slot == 0, local == ATOM_DEV - 1), HALO, offset)
    return (HALO + local + offset).astype(jnp.int32)


def place_ends(values, key, least, high):
    place = [jax.random.randint(jax.random.fold_in(key, axis), (), 0, length) for axis, length in enumerate(values.shape)]
    widest = values.shape.index(max(values.shape))
    next_to = place[:widest] + [(place[widest] + 1) % values.shape[widest]] + place[widest + 1:]
    return values.at[tuple(place)].set(least).at[tuple(next_to)].set(high)


def centred(rng, shape, spread, most, held_as=jnp.bfloat16):
    drawn = spread * jax.random.normal(rng, shape, jnp.float32)
    return jnp.clip(drawn, min=-most, max=most).astype(held_as)


def setup_inputs(seed: int = 0) -> dict:
    key_of = jax.random.split(jax.random.key(seed), 13)
    positions = draw_positions(jax.random.fold_in(key_of[12], 71), 0)
    species = place_ends(jax.random.randint(key_of[1], (ATOMS,), 0, SPECIES), jax.random.fold_in(key_of[1], 1), 0, SPECIES - 1).astype(jnp.int32)
    counts = draw_counts(jax.random.fold_in(key_of[12], 71), 0)
    neighbours = draw_neighbours(jax.random.fold_in(key_of[12], 71), 0)
    send_list = place_ends(jax.random.randint(key_of[4], (2 * HALO * N_ATOM,), 0, ATOM_DEV), jax.random.fold_in(key_of[4], 1), 0, ATOM_DEV - 1).astype(jnp.int32)
    climb = place_ends((jax.random.randint(key_of[5], (IMAGES,), 0, 2) < 1).astype(jnp.int32), jax.random.fold_in(key_of[5], 1), 0, 1)
    embed = centred(key_of[6], (SPECIES, C), 1.0, 6.0)
    ref_energy = jnp.clip(jax.random.uniform(key_of[7], (SPECIES,), jnp.float32, -2.0, 2.0), -2.0, 2.0)
    rad_in = centred(key_of[8], (LAYERS + 1, NB, RAD), 4.0, 24.0)
    rad_out = centred(key_of[9], (LAYERS + 1, RAD, C), 0.008, 0.047851562)
    mixing = centred(key_of[10], (LAYERS, C, C), C ** -0.5, 0.5)
    w_energy = centred(key_of[11], (C,), C ** -0.5, 0.5)
    return {"positions": positions, "species": species, "counts": counts, "neighbours": neighbours, "send_list": send_list, "climb": climb, "embed": embed, "ref_energy": ref_energy, "rad_in": rad_in, "rad_out": rad_out, "mixing": mixing, "w_energy": w_energy}


spring_constant = 5.0

def radial_field(basis, w_in, w_out):
    hidden = lax.dot_general(w_in, basis, (((0,), (0,)), ((), ())), preferred_element_type=jnp.float32)
    hidden = jax.nn.silu(hidden).astype(jnp.bfloat16)
    return lax.dot_general(hidden, w_out, (((0,), (0,)), ((), ())), preferred_element_type=jnp.float32)

def species_table(kinds, embed):
    onehot = (kinds[:, None] == jnp.arange(SPECIES, dtype=jnp.int32)[None, :]).astype(jnp.bfloat16)
    return jnp.dot(onehot, embed, preferred_element_type=jnp.float32).astype(jnp.bfloat16)

def to_tiles(arr):
    lead = arr.shape[:-1]
    arr = arr.reshape(lead + (N_ATOM, ATOM_DEV))
    return jnp.moveaxis(arr, -2, 0)

def reference(positions, species, counts, neighbours, send_list, climb, embed, ref_energy, rad_in, rad_out, mixing, w_energy):
    lists = send_list.reshape(N_ATOM, 2 * HALO)
    starts = (jnp.arange(N_ATOM, dtype=jnp.int32) * ATOM_DEV)[:, None]
    glob = lists + starts
    lower = jnp.roll(glob[:, HALO:], 1, axis=0)
    upper = jnp.roll(glob[:, :HALO], -1, axis=0)
    local = starts + jnp.arange(ATOM_DEV, dtype=jnp.int32)[None, :]
    tables = jnp.concatenate([lower, local, upper], axis=1)
    tiled = to_tiles(neighbours).reshape(N_ATOM, NBR * ATOM_DEV)
    partner = jnp.take_along_axis(tables, tiled, axis=1).reshape(N_ATOM, NBR, ATOM_DEV)
    partner = jnp.moveaxis(partner, 0, 1).reshape(NBR, ATOMS)
    slots = lax.broadcasted_iota(jnp.int32, (NBR, ATOMS), 0)
    live = (slots < counts[None, :]).astype(jnp.float32)
    centres = 2.0 * jnp.arange(NB, dtype=jnp.float32)
    onehot_ref = jnp.where(species[:, None] == jnp.arange(SPECIES, dtype=jnp.int32)[None, :], ref_energy[None, :], jnp.float32(0.0))
    atom_ref = lax.optimization_barrier(jnp.sum(onehot_ref, axis=1))
    forces = []
    energies = []
    for image in range(IMAGES):
        coords = positions[image]
        delta = coords[:, partner] - coords[:, None, :]
        dist_sq = lax.optimization_barrier(jnp.sum(delta * delta, axis=0))
        basis = jnp.exp(-jnp.square(dist_sq[None] - centres[:, None, None]) / 8.0).astype(jnp.bfloat16)
        basis_tiles = to_tiles(basis).reshape(N_ATOM, NB, NBR * ATOM_DEV)
        partner_tiles = to_tiles(partner)
        live_tiles = to_tiles(live)
        delta_tiles = to_tiles(delta)
        feats = species_table(species, embed)
        for layer in range(LAYERS):

            def step(items, table=feats, layer=layer):
                nbr_b, basis_b, live_b, feats_b = items
                field = radial_field(basis_b, rad_in[layer], rad_out[layer]).reshape(NBR, ATOM_DEV, C)
                far = table[nbr_b].astype(jnp.float32)
                summed = lax.optimization_barrier(jnp.sum(field * far * live_b[:, :, None], axis=0))
                scaled = (summed / math.sqrt(NBR)).astype(jnp.bfloat16)
                update = jax.nn.silu(jnp.dot(scaled, mixing[layer], preferred_element_type=jnp.float32))
                return (feats_b.astype(jnp.float32) + update).astype(jnp.bfloat16)
            feats = lax.map(step, (partner_tiles, basis_tiles, live_tiles, feats.reshape(N_ATOM, ATOM_DEV, C))).reshape(ATOMS, C)

        def force_step(items, table=feats):
            nbr_b, basis_b, live_b, feats_b, delta_b = items
            field = radial_field(basis_b, rad_in[LAYERS], rad_out[LAYERS]).reshape(NBR, ATOM_DEV, C)
            far = table[nbr_b].astype(jnp.float32)
            near = feats_b.astype(jnp.float32)[None]
            pair = lax.optimization_barrier(jnp.sum(field * near * far, axis=2)) * (live_b / math.sqrt(C))
            return lax.optimization_barrier(jnp.sum(pair[None] * delta_b, axis=1))
        force_tiles = lax.map(force_step, (partner_tiles, basis_tiles, live_tiles, feats.reshape(N_ATOM, ATOM_DEV, C), delta_tiles))
        forces.append(jnp.moveaxis(force_tiles, 0, 1).reshape(3, ATOMS))
        per_atom = jnp.dot(feats, w_energy, preferred_element_type=jnp.float32) + atom_ref
        energies.append(jnp.sum(per_atom) / ATOMS)
    outputs = []
    for image in range(IMAGES):
        force = forces[image]
        if image == 0 or image == IMAGES - 1:
            outputs.append(force)
        else:
            back = positions[image] - positions[image - 1]
            fore = positions[image + 1] - positions[image]
            back_len = jnp.sqrt(jnp.sum(back * back) + 1e-06)
            fore_len = jnp.sqrt(jnp.sum(fore * fore) + 1e-06)
            tangent = back / back_len + fore / fore_len
            tau_sq = jnp.sum(tangent * tangent)
            along = jnp.sum(force * tangent)
            proj = along / tau_sq
            interior = force - proj * tangent + spring_constant * (fore_len - back_len) / jnp.sqrt(tau_sq) * tangent
            climbing = force - 2.0 * proj * tangent
            outputs.append(jnp.where(climb[image] == 1, climbing, interior))
    return (jnp.stack(outputs, axis=0), jnp.stack(energies, axis=0))
```

```python
import functools
import math

import jax
import jax.numpy as jnp
from jax import lax
from jax.experimental import pallas as pl
from jax.experimental.pallas import tpu as pltpu
from jax.sharding import PartitionSpec as P

F32 = jnp.float32
BF16 = jnp.bfloat16
I32 = jnp.int32
MESH = pl.DeviceIdType.MESH

SPRING = 5.0
C = 128
RAD = 64
NB = 8
SPECIES = 4
FAN = 16
HALO = 256
ATOMS = 1024
BLK = 256
BLOCKS = ATOMS // BLK
WIN = BLK + 2 * HALO
TABLE = ATOMS + 2 * HALO
LANES = 128
FAR_AWAY = 1.0e4


def lane_gather(source, index):
    return jnp.take_along_axis(source, index, axis=1, mode="promise_in_bounds")


def dot(a, b):
    return jnp.dot(a, b, preferred_element_type=F32)


def total(x):
    return jnp.sum(jnp.sum(x, axis=0, keepdims=True), axis=1, keepdims=True)


def one_hot_rows(index, tile, iota):
    local = index - float(256 * tile)
    inside = jnp.logical_and(local >= 0.0, local < 256.0)
    local = jnp.where(inside, local, -1.0)
    local = jnp.broadcast_to(local, (16, local.shape[1])).astype(BF16)
    local = jnp.concatenate([local] * 16, axis=0)
    return jnp.where(local == iota, jnp.ones_like(iota), jnp.zeros_like(iota))


def kernel(
    n_img,
    n_atom,
    pos,
    species,
    counts,
    neighbours,
    send_list,
    climb,
    embed,
    ref_energy,
    rad_in,
    rad_out,
    mixing,
    w_energy,
    out,
    energy_out,
    ptab,
    sendpos,
    band,
    t1,
    t2,
    sendh,
    onehot,
    sendhot,
    iota_ref,
    hid,
    masked,
    w_hid,
    w_first,
    rad_t,
    mix_t,
    emb_t,
    basis,
    sp_mask,
    sp_far,
    delta,
    force,
    rbuf,
    pos_send,
    pos_recv,
    img_send,
    img_recv,
    h_send,
    h_recv,
    r_send,
    r_recv,
):
    img = lax.axis_index("img")
    me = lax.axis_index("atom")
    up = lax.rem(me + 1, n_atom)
    down = lax.rem(me + n_atom - 1, n_atom)
    img_up = lax.rem(img + 1, n_img)
    img_down = lax.rem(img + n_img - 1, n_img)

    barrier = pltpu.get_barrier_semaphore()

    def greet(d, _):
        peer = lax.rem(me + d, n_atom)
        pl.semaphore_signal(barrier, inc=1, device_id=(img, peer), device_id_type=MESH)
        return 0

    lax.fori_loop(1, n_atom, greet, 0)
    for other in (img_up, img_down):
        pl.semaphore_signal(barrier, inc=1, device_id=(other, me), device_id_type=MESH)

    ptab[0:3, HALO : HALO + ATOMS] = pos[0]
    ptab[3:4, HALO : HALO + ATOMS] = species[...].astype(F32)
    ptab[4:8, HALO : HALO + ATOMS] = jnp.zeros((4, ATOMS), F32)
    for t in range(4):
        index = jnp.broadcast_to(send_list[:, t * LANES : (t + 1) * LANES], (8, LANES))
        low = index & 127
        high = index >> 7
        got = jnp.zeros((8, LANES), F32)
        for w in range(ATOMS // LANES):
            source = ptab[:, HALO + w * LANES : HALO + (w + 1) * LANES]
            got = jnp.where(high == w, lane_gather(source, low), got)
        sendpos[:, t * LANES : (t + 1) * LANES] = got

    row = lax.broadcasted_iota(I32, (256, BLK), 0).astype(F32).astype(BF16)
    iota_ref[...] = row
    for layer in range(3):
        rad_t[layer] = rad_out[layer].astype(F32).T.astype(BF16)
    for layer in range(2):
        mix_t[layer] = mixing[layer].astype(F32).T.astype(BF16)
    emb = embed[...].astype(F32)
    emb_rows = jnp.concatenate([emb, jnp.zeros((C - SPECIES, C), F32)], axis=0)
    emb_t[...] = emb_rows.T.astype(BF16)
    first = rad_out[0].astype(F32)
    w0 = jnp.concatenate([first * emb[k : k + 1, :] for k in range(SPECIES)], axis=0).T.astype(BF16)
    for s in range(FAN):
        w_first[:, s * 256 : (s + 1) * 256] = w0
    lane = lax.broadcasted_iota(I32, (NB, C), 1)
    spread = (lane // FAN == lax.broadcasted_iota(I32, (NB, C), 0)).astype(F32).astype(BF16)
    lane64 = lax.broadcasted_iota(I32, (RAD, C), 1) % FAN
    for layer in range(3):
        wide = lax.dot_general(
            rad_in[layer], spread, (((0,), (0,)), ((), ())), preferred_element_type=F32
        )
        wide = wide * 0.5
        for s in range(FAN):
            start = s * 192 + layer * RAD
            w_hid[start : start + RAD, :] = jnp.where(lane64 == s, wide, 0.0).astype(BF16)

    def send_row(t, slot, target):
        return pltpu.make_async_remote_copy(
            src_ref=t[0],
            dst_ref=t[1],
            send_sem=t[2].at[slot],
            recv_sem=t[3].at[slot],
            device_id=target,
            device_id_type=MESH,
        )

    def pos_copies():
        return (
            send_row(
                (sendpos.at[:, 0:HALO], ptab.at[:, HALO + ATOMS : TABLE], pos_send, pos_recv),
                0,
                (img, down),
            ),
            send_row(
                (sendpos.at[:, HALO : 2 * HALO], ptab.at[:, 0:HALO], pos_send, pos_recv),
                1,
                (img, up),
            ),
        )

    def img_copies():
        return (
            send_row((pos.at[0], band.at[0], img_send, img_recv), 0, (img_up, me)),
            send_row((pos.at[0], band.at[1], img_send, img_recv), 1, (img_down, me)),
        )

    def h_copies(phase, table):
        return (
            send_row(
                (
                    sendh.at[phase, :, 0:HALO],
                    table.at[:, HALO + ATOMS : TABLE],
                    h_send.at[phase],
                    h_recv.at[phase],
                ),
                0,
                (img, down),
            ),
            send_row(
                (
                    sendh.at[phase, :, HALO : 2 * HALO],
                    table.at[:, 0:HALO],
                    h_send.at[phase],
                    h_recv.at[phase],
                ),
                1,
                (img, up),
            ),
        )

    lane_row = lax.broadcasted_iota(I32, (1, LANES), 1)

    def reduce_start(phase, values):
        message = jnp.zeros((1, LANES), F32)
        for n, value in enumerate(values):
            message = jnp.where(lane_row == n, value, message)
        rbuf[phase, me] = message

        def each(d, _):
            peer = lax.rem(me + d, n_atom)
            pltpu.make_async_remote_copy(
                src_ref=rbuf.at[phase, me],
                dst_ref=rbuf.at[phase, me],
                send_sem=r_send.at[phase, peer],
                recv_sem=r_recv.at[phase, me],
                device_id=(img, peer),
                device_id_type=MESH,
            ).start()
            return 0

        lax.fori_loop(1, n_atom, each, 0)

    def reduce_wait(phase, number):
        def each(d, _):
            peer = lax.rem(me + d, n_atom)
            copy = pltpu.make_async_remote_copy(
                src_ref=rbuf.at[phase, me],
                dst_ref=rbuf.at[phase, peer],
                send_sem=r_send.at[phase, peer],
                recv_sem=r_recv.at[phase, peer],
                device_id=(img, peer),
                device_id_type=MESH,
            )
            copy.wait_send()
            copy.wait_recv()
            return 0

        lax.fori_loop(1, n_atom, each, 0)
        summed = jnp.sum(rbuf[phase], axis=0)
        return [
            jnp.sum(jnp.where(lane_row == n, summed, 0.0), axis=1, keepdims=True)
            for n in range(number)
        ]

    def order(i):
        return lax.rem(i + 1, BLOCKS)

    def first_block(i, _):
        block = order(i)
        start = pl.multiple_of(block * BLK, BLK)

        @pl.when(i == 1)
        def _():
            pl.semaphore_wait(barrier, n_atom + 1)
            for copy in pos_copies() + img_copies():
                copy.start()

        @pl.when(i == 2)
        def _():
            for copy in pos_copies() + img_copies():
                copy.wait()
            here = pos[0]
            behind = here - band[0]
            ahead = band[1] - here
            reduce_start(0, (total(behind * behind), total(ahead * ahead)))

        for t in range(BLK // LANES):
            at = pl.multiple_of(start + t * LANES, LANES)
            offset = neighbours[:, pl.ds(at, LANES)] - at
            low = offset & 127
            high = offset >> 7
            got = [None] * 4
            for w in range(WIN // LANES - 1):
                for comp in range(4):
                    source = jnp.broadcast_to(
                        ptab[comp : comp + 1, pl.ds(pl.multiple_of(at + w * LANES, LANES), LANES)],
                        (FAN, LANES),
                    )
                    value = lane_gather(source, low)
                    got[comp] = value if w == 0 else jnp.where(high == w, value, got[comp])
            slots = lax.broadcasted_iota(I32, (FAN, LANES), 0)
            live = slots < counts[:, pl.ds(at, LANES)]
            dist = jnp.zeros((FAN, LANES), F32)
            for comp in range(3):
                diff = got[comp] - pos[0, comp : comp + 1, pl.ds(at, LANES)]
                delta[comp, :, pl.ds(at, LANES)] = diff
                dist = dist + diff * diff
            dist = jnp.where(live, dist, FAR_AWAY)
            for k in range(NB):
                shifted = dist - 2.0 * k
                basis[k * FAN : (k + 1) * FAN, t * LANES : (t + 1) * LANES] = jnp.exp(
                    -(shifted * shifted) / 8.0
                ).astype(BF16)
            for k in range(SPECIES):
                sp_mask[k, :, t * LANES : (t + 1) * LANES] = (got[3] == float(k)).astype(F32)

        def slot(s, _):
            rows = pl.multiple_of(s * 192, 192)
            half = dot(w_hid[pl.ds(rows, 192), :], basis[...])
            unit = (half + half * jnp.tanh(half)).astype(BF16)
            at_row = pl.multiple_of(s * RAD, RAD)
            for layer in (1, 2):
                hid[layer - 1, pl.ds(at_row, RAD), pl.ds(start, BLK)] = unit[
                    layer * RAD : (layer + 1) * RAD
                ]
            for k in range(SPECIES):
                mask = jnp.broadcast_to(sp_mask[k, pl.ds(s, 1), :], (16, BLK)).astype(BF16)
                mask = jnp.concatenate([mask] * (RAD // 16), axis=0)
                masked[pl.ds(pl.multiple_of(s * 256 + k * RAD, RAD), RAD), :] = unit[:RAD] * mask
            index = (neighbours[pl.ds(s, 1), pl.ds(start, BLK)] - start).astype(F32)
            for tile in range(WIN // 256):
                onehot[
                    block,
                    tile * 256 : (tile + 1) * 256,
                    pl.ds(pl.multiple_of(s * BLK, BLK), BLK),
                ] = one_hot_rows(index, tile, iota_ref[...])
            return 0

        lax.fori_loop(0, FAN, slot, 0, unroll=2)
        summed = dot(w_first[...], masked[...])
        scaled = (summed / math.sqrt(FAN)).astype(BF16)
        half = dot(mix_t[0], scaled) * 0.5
        kinds = jnp.broadcast_to(species[:, pl.ds(start, BLK)], (16, BLK))
        own_hot = (kinds == lax.broadcasted_iota(I32, (16, BLK), 0)).astype(F32).astype(BF16)
        h0 = dot(emb_t[:, :16], own_hot)
        t1[:, pl.ds(pl.multiple_of(start + HALO, BLK), BLK)] = (
            h0 + (half + half * jnp.tanh(half))
        ).astype(BF16)
        return 0

    lax.fori_loop(0, BLOCKS, first_block, 0)

    for tile in range(ATOMS // 256):
        for side in range(2):
            cols = slice(side * HALO, (side + 1) * HALO)
            sendhot[tile * 256 : (tile + 1) * 256, cols] = one_hot_rows(
                send_list[:, cols].astype(F32), tile, iota_ref[...]
            )

    def lend(phase, table):
        sendh[phase] = dot(table[:, HALO : HALO + ATOMS], sendhot[...]).astype(BF16)

    lend(0, t1)
    back_sq, fore_sq = reduce_wait(0, 2)
    back_len = jnp.sqrt(back_sq + 1e-06)
    fore_len = jnp.sqrt(fore_sq + 1e-06)
    here = pos[0]
    tangent = (here - band[0]) / back_len + (band[1] - here) / fore_len
    for copy in h_copies(0, t1):
        copy.start()
    reduce_start(1, (total(tangent * tangent),))

    def second_block(i, _):
        block = order(i)
        start = pl.multiple_of(block * BLK, BLK)

        @pl.when(i == 2)
        def _():
            for copy in h_copies(0, t1):
                copy.wait()

        def slot(s, acc):
            near = t1[:, pl.ds(start, WIN)]
            far = dot(near, onehot[block, :, pl.ds(pl.multiple_of(s * BLK, BLK), BLK)])
            field = dot(rad_t[1], hid[0, pl.ds(pl.multiple_of(s * RAD, RAD), RAD), pl.ds(start, BLK)])
            return acc + far * field

        summed = lax.fori_loop(0, FAN, slot, jnp.zeros((C, BLK), F32), unroll=2)
        scaled = (summed / math.sqrt(FAN)).astype(BF16)
        half = dot(mix_t[1], scaled) * 0.5
        own = pl.ds(pl.multiple_of(start + HALO, BLK), BLK)
        t2[:, own] = (t1[:, own].astype(F32) + (half + half * jnp.tanh(half))).astype(BF16)
        return 0

    lax.fori_loop(0, BLOCKS, second_block, 0)
    lend(1, t2)
    (tau_sq,) = reduce_wait(1, 1)
    for copy in h_copies(1, t2):
        copy.start()

    def force_block(i, _):
        block = order(i)
        start = pl.multiple_of(block * BLK, BLK)

        @pl.when(i == 2)
        def _():
            for copy in h_copies(1, t2):
                copy.wait()

        own = t2[:, pl.ds(pl.multiple_of(start + HALO, BLK), BLK)].astype(F32)

        def slot(s, acc):
            near = t2[:, pl.ds(start, WIN)]
            far = dot(near, onehot[block, :, pl.ds(pl.multiple_of(s * BLK, BLK), BLK)])
            field = dot(rad_t[2], hid[1, pl.ds(pl.multiple_of(s * RAD, RAD), RAD), pl.ds(start, BLK)])
            pair = jnp.sum(field * own * far, axis=0, keepdims=True)
            return tuple(
                acc[comp] + pair * delta[comp, pl.ds(s, 1), pl.ds(start, BLK)] for comp in range(3)
            )

        zero = jnp.zeros((1, BLK), F32)
        parts = lax.fori_loop(0, FAN, slot, (zero, zero, zero), unroll=2)
        for comp in range(3):
            force[comp : comp + 1, pl.ds(start, BLK)] = parts[comp] * (1.0 / math.sqrt(C))
        return 0

    lax.fori_loop(0, BLOCKS, force_block, 0)

    per_atom = dot(jnp.broadcast_to(w_energy[...], (16, C)), t2[:, HALO : HALO + ATOMS])[0:1, :]
    for k in range(SPECIES):
        per_atom = per_atom + jnp.where(species[...] == k, ref_energy[k], 0.0)
    pull = force[0:3, :]
    reduce_start(
        2, (jnp.sum(per_atom, axis=1, keepdims=True), total(pull * tangent))
    )
    energy, along = reduce_wait(2, 2)
    energy_out[...] = energy / (ATOMS * n_atom)
    proj = along / tau_sq
    interior = (
        pull - proj * tangent + SPRING * (fore_len - back_len) / jnp.sqrt(tau_sq) * tangent
    )
    climbing = pull - 2.0 * proj * tangent
    is_end = jnp.logical_or(img == 0, img == n_img - 1)
    band_force = jnp.where(climb[...] == 1, climbing, interior)
    out[0] = jnp.where(is_end, pull, band_force)


def on_device(
    n_img,
    n_atom,
    positions,
    species,
    counts,
    neighbours,
    send_list,
    climb,
    embed,
    ref_energy,
    rad_in,
    rad_out,
    mixing,
    w_energy,
):
    vmem = pl.BlockSpec(memory_space=pltpu.VMEM)
    smem = pl.BlockSpec(memory_space=pltpu.SMEM)
    dma = pltpu.SemaphoreType.DMA
    result, energy = pl.pallas_call(
        functools.partial(kernel, n_img, n_atom),
        out_shape=(
            jax.ShapeDtypeStruct((1, 3, ATOMS), F32),
            jax.ShapeDtypeStruct((1, 1), F32),
        ),
        in_specs=[vmem, vmem, vmem, vmem, vmem, vmem, vmem, smem, vmem, vmem, vmem, vmem],
        out_specs=(vmem, vmem),
        scratch_shapes=[
            pltpu.VMEM((8, TABLE), F32),
            pltpu.VMEM((8, 2 * HALO), F32),
            pltpu.VMEM((2, 3, ATOMS), F32),
            pltpu.VMEM((C, TABLE), BF16),
            pltpu.VMEM((C, TABLE), BF16),
            pltpu.VMEM((2, C, 2 * HALO), BF16),
            pltpu.VMEM((BLOCKS, WIN, FAN * BLK), BF16),
            pltpu.VMEM((ATOMS, 2 * HALO), BF16),
            pltpu.VMEM((256, BLK), BF16),
            pltpu.VMEM((2, FAN * RAD, ATOMS), BF16),
            pltpu.VMEM((FAN * 256, BLK), BF16),
            pltpu.VMEM((FAN * 192, C), BF16),
            pltpu.VMEM((C, FAN * 256), BF16),
            pltpu.VMEM((3, C, RAD), BF16),
            pltpu.VMEM((2, C, C), BF16),
            pltpu.VMEM((C, C), BF16),
            pltpu.VMEM((C, BLK), BF16),
            pltpu.VMEM((SPECIES, FAN, BLK), F32),
            pltpu.VMEM((FAN, BLK), F32),
            pltpu.VMEM((3, FAN, ATOMS), F32),
            pltpu.VMEM((8, ATOMS), F32),
            pltpu.VMEM((3, n_atom, 1, LANES), F32),
            dma((2,)),
            dma((2,)),
            dma((2,)),
            dma((2,)),
            dma((2, 2)),
            dma((2, 2)),
            dma((3, n_atom)),
            dma((3, n_atom)),
        ],
        compiler_params=pltpu.CompilerParams(
            collective_id=0, has_side_effects=True, vmem_limit_bytes=60 * 1024 * 1024
        ),
        name="band_step",
    )(
        positions,
        species.reshape(1, ATOMS),
        counts.reshape(1, ATOMS),
        neighbours,
        send_list.reshape(1, 2 * HALO),
        climb.reshape(1, 1),
        embed,
        ref_energy,
        rad_in,
        rad_out,
        mixing,
        w_energy.reshape(1, C),
    )
    return result, energy.reshape(1)


def solution(mesh):
    return jax.shard_map(
        functools.partial(on_device, mesh.shape["img"], mesh.shape["atom"]),
        mesh=mesh,
        in_specs=(
            P("img", None, "atom"),
            P("atom"),
            P("atom"),
            P(None, "atom"),
            P("atom"),
            P("img"),
            P(),
            P(),
            P(),
            P(),
            P(),
            P(),
        ),
        out_specs=(P("img", None, "atom"), P("img")),
        check_vma=False,
    )
```

```python
import functools
import math

import jax
import jax.numpy as jnp
from jax import lax
from jax.experimental import pallas as pl
from jax.experimental.pallas import tpu as pltpu
from jax.sharding import PartitionSpec as P

F32 = jnp.float32
BF16 = jnp.bfloat16
I32 = jnp.int32
MESH = pl.DeviceIdType.MESH

SPRING = 5.0
C = 128
RAD = 64
NB = 8
SPECIES = 4
FAN = 16
HALO = 256
ATOMS = 1024
BLK = 256
BLOCKS = ATOMS // BLK
LANES = 128
WIN = LANES + 2 * HALO
TILES = ATOMS // LANES
TABLE = ATOMS + 2 * HALO
UNROLL = 4
FAR_AWAY = 1.0e4


def lane_gather(source, index):
    return jnp.take_along_axis(source, index, axis=1, mode="promise_in_bounds")


def dot(a, b):
    return jnp.dot(a, b, preferred_element_type=F32)


def total(x):
    return jnp.sum(jnp.sum(x, axis=0, keepdims=True), axis=1, keepdims=True)


def one_hot_rows(local, iota):
    local = jnp.broadcast_to(local, (16, LANES)).astype(BF16)
    local = jnp.concatenate([local] * 16, axis=0)
    return jnp.where(local == iota, jnp.ones_like(iota), jnp.zeros_like(iota))


def side_by_side(left, right):
    return jnp.concatenate([left, right], axis=1)


def tile_of(lane):
    return slice(lane * LANES, (lane + 1) * LANES)


def kernel(
    n_img,
    n_atom,
    pos,
    species,
    counts,
    neighbours,
    send_list,
    climb,
    embed,
    ref_energy,
    rad_in,
    rad_out,
    mixing,
    w_energy,
    out,
    energy_out,
    ptab,
    sendpos,
    band,
    t1,
    t2,
    sendh,
    onehot,
    sendhot,
    iota_ref,
    hid,
    masked,
    w_hid,
    w_first,
    rad_t,
    mix_t,
    emb_t,
    basis,
    sp_mask,
    delta,
    rel,
    scaled_ref,
    last_ref,
    own_ref,
    force,
    tang,
    rbuf,
    pos_send,
    pos_recv,
    img_send,
    img_recv,
    h_send,
    h_recv,
    r_send,
    r_recv,
):
    img = lax.axis_index("img")
    me = lax.axis_index("atom")

    def ring(index, step, size):
        moved = index + step
        return jnp.where(moved >= size, moved - size, moved)

    up = ring(me, 1, n_atom)
    down = ring(me, n_atom - 1, n_atom)
    img_up = ring(img, 1, n_img)
    img_down = ring(img, n_img - 1, n_img)

    barrier = pltpu.get_barrier_semaphore()
    for d in range(1, n_atom):
        pl.semaphore_signal(
            barrier, inc=1, device_id=(img, ring(me, d, n_atom)), device_id_type=MESH
        )
    for other in (img_up, img_down):
        pl.semaphore_signal(barrier, inc=1, device_id=(other, me), device_id_type=MESH)

    own_cols = slice(HALO, HALO + ATOMS)
    for comp in range(3):
        ptab[comp : comp + 1, own_cols] = pos[comp]
    ptab[3:4, own_cols] = species[...].astype(F32)
    ptab[4:8, own_cols] = jnp.zeros((4, ATOMS), F32)
    for t in range(4):
        index = jnp.broadcast_to(send_list[:, tile_of(t)], (8, LANES))
        low = index & 127
        high = index >> 7
        got = jnp.zeros((8, LANES), F32)
        for w in range(ATOMS // LANES):
            source = ptab[:, HALO + w * LANES : HALO + (w + 1) * LANES]
            got = jnp.where(high == w, lane_gather(source, low), got)
        sendpos[:, tile_of(t)] = got

    iota_ref[...] = lax.broadcasted_iota(I32, (256, LANES), 0).astype(F32).astype(BF16)
    for layer in range(3):
        rad_t[layer] = rad_out[layer].astype(F32).T.astype(BF16)
    for layer in range(2):
        mix_t[layer] = mixing[layer].astype(F32).T.astype(BF16)
    emb = embed[...].astype(F32)
    emb_rows = jnp.concatenate([emb, jnp.zeros((C - SPECIES, C), F32)], axis=0)
    emb_t[...] = emb_rows.T.astype(BF16)
    first = rad_out[0].astype(F32)
    w0 = jnp.concatenate([first * emb[k : k + 1, :] for k in range(SPECIES)], axis=0).T.astype(BF16)
    for s in range(FAN):
        w_first[:, s * 256 : (s + 1) * 256] = w0
    lane = lax.broadcasted_iota(I32, (NB, C), 1)
    spread = (lane // FAN == lax.broadcasted_iota(I32, (NB, C), 0)).astype(F32).astype(BF16)
    lane64 = lax.broadcasted_iota(I32, (RAD, C), 1) % FAN
    for layer in range(3):
        wide = lax.dot_general(
            rad_in[layer], spread, (((0,), (0,)), ((), ())), preferred_element_type=F32
        )
        wide = wide * 0.5
        for s in range(FAN):
            start = s * 192 + layer * RAD
            w_hid[start : start + RAD, :] = jnp.where(lane64 == s, wide, 0.0).astype(BF16)

    def copy_to(source, target, send, recv, device):
        return pltpu.make_async_remote_copy(
            src_ref=source,
            dst_ref=target,
            send_sem=send,
            recv_sem=recv,
            device_id=device,
            device_id_type=MESH,
        )

    def pos_copies():
        low, high = slice(0, HALO), slice(HALO + ATOMS, TABLE)
        return (
            copy_to(
                sendpos.at[:, 0:HALO], ptab.at[:, high], pos_send.at[0], pos_recv.at[0], (img, down)
            ),
            copy_to(
                sendpos.at[:, HALO : 2 * HALO],
                ptab.at[:, low],
                pos_send.at[1],
                pos_recv.at[1],
                (img, up),
            ),
        )

    def img_copies():
        return (
            copy_to(pos, band.at[0], img_send.at[0], img_recv.at[0], (img_up, me)),
            copy_to(pos, band.at[1], img_send.at[1], img_recv.at[1], (img_down, me)),
        )

    def h_copies(phase, table):
        return (
            copy_to(
                sendh.at[phase, 0:2],
                table.at[10:12],
                h_send.at[phase, 0],
                h_recv.at[phase, 0],
                (img, down),
            ),
            copy_to(
                sendh.at[phase, 2:4],
                table.at[0:2],
                h_send.at[phase, 1],
                h_recv.at[phase, 1],
                (img, up),
            ),
        )

    lane_row = lax.broadcasted_iota(I32, (1, LANES), 1)

    def reduce_start(phase, values):
        message = jnp.zeros((1, LANES), F32)
        for n, value in enumerate(values):
            message = jnp.where(lane_row == n, value, message)
        rbuf[phase, me] = message
        for d in range(1, n_atom):
            copy_to(
                rbuf.at[phase, me],
                rbuf.at[phase, me],
                r_send.at[phase],
                r_recv.at[phase],
                (img, ring(me, d, n_atom)),
            ).start()

    def reduce_wait(phase, number):
        others = rbuf.at[phase, 0 : n_atom - 1]
        arrived = copy_to(others, others, r_send.at[phase], r_recv.at[phase], (img, up))
        arrived.wait_send()
        arrived.wait_recv()
        summed = jnp.sum(rbuf[phase], axis=0)
        return [
            jnp.sum(jnp.where(lane_row == n, summed, 0.0), axis=1, keepdims=True)
            for n in range(number)
        ]

    def first_block(i, _):
        block = lax.rem(i + 1, BLOCKS)
        start = pl.multiple_of(block * BLK, BLK)

        @pl.when(i == 1)
        def _():
            pl.semaphore_wait(barrier, n_atom + 1)
            for copy in pos_copies() + img_copies():
                copy.start()

        @pl.when(i == 2)
        def _():
            for copy in pos_copies() + img_copies():
                copy.wait()
            behind = pos[...] - band[0]
            ahead = band[1] - pos[...]
            reduce_start(
                0, (total(jnp.sum(behind * behind, axis=0)), total(jnp.sum(ahead * ahead, axis=0)))
            )

        for t in range(BLK // LANES):
            at = pl.multiple_of(start + t * LANES, LANES)
            tile = block * 2 + t
            offset = neighbours[:, pl.ds(at, LANES)] - at
            rel[tile] = offset
            low = offset & 127
            high = offset >> 7
            got = [None] * 4
            for w in range(WIN // LANES):
                here = high == w
                for comp in range(4):
                    source = jnp.broadcast_to(
                        ptab[comp : comp + 1, pl.ds(pl.multiple_of(at + w * LANES, LANES), LANES)],
                        (FAN, LANES),
                    )
                    value = lane_gather(source, low)
                    got[comp] = value if w == 0 else jnp.where(here, value, got[comp])
            slots = lax.broadcasted_iota(I32, (FAN, LANES), 0)
            live = slots < counts[:, pl.ds(at, LANES)]
            dist = jnp.zeros((FAN, LANES), F32)
            for comp in range(3):
                diff = got[comp] - pos[comp, :, pl.ds(at, LANES)]
                delta[comp, tile] = diff
                dist = dist + diff * diff
            dist = jnp.where(live, dist, FAR_AWAY)
            for k in range(NB):
                shifted = dist - 2.0 * k
                basis[t, k * FAN : (k + 1) * FAN, :] = jnp.exp(-(shifted * shifted) / 8.0).astype(
                    BF16
                )
            for k in range(SPECIES):
                sp_mask[t, k] = (got[3] == float(k)).astype(F32)

        def slot(s, _):
            rows = pl.multiple_of(s * 192, 192)
            half = dot(w_hid[pl.ds(rows, 192), :], side_by_side(basis[0], basis[1]))
            unit = (half + half * jnp.tanh(half)).astype(BF16)
            at_row = pl.multiple_of(s * RAD, RAD)
            for t in range(BLK // LANES):
                tile = block * 2 + t
                for layer in (1, 2):
                    hid[layer - 1, tile, pl.ds(at_row, RAD), :] = unit[
                        layer * RAD : (layer + 1) * RAD, tile_of(t)
                    ]
                for k in range(SPECIES):
                    mask = jnp.broadcast_to(sp_mask[t, k, pl.ds(s, 1), :], (16, LANES)).astype(BF16)
                    mask = jnp.concatenate([mask] * (RAD // 16), axis=0)
                    masked[t, pl.ds(pl.multiple_of(s * 256 + k * RAD, RAD), RAD), :] = (
                        unit[:RAD, tile_of(t)] * mask
                    )
                index = rel[tile, pl.ds(s, 1), :] & 255
                onehot[tile, s] = one_hot_rows(index.astype(F32), iota_ref[...])
            return 0

        lax.fori_loop(0, FAN, slot, 0, unroll=2)
        summed = dot(w_first[...], side_by_side(masked[0], masked[1]))
        scaled = (summed / math.sqrt(FAN)).astype(BF16)
        half = dot(mix_t[0], scaled) * 0.5
        kinds = jnp.broadcast_to(species[:, pl.ds(start, BLK)], (16, BLK))
        own_hot = (kinds == lax.broadcasted_iota(I32, (16, BLK), 0)).astype(F32).astype(BF16)
        h1 = (dot(emb_t[:, :16], own_hot) + (half + half * jnp.tanh(half))).astype(BF16)
        for t in range(BLK // LANES):
            t1[block * 2 + t + 2] = h1[:, tile_of(t)]
        return 0

    lax.fori_loop(0, BLOCKS, first_block, 0)

    for t in range(2 * HALO // LANES):
        index = send_list[:, tile_of(t)].astype(F32)
        for part in range(ATOMS // 256):
            local = index - 256.0 * part
            inside = jnp.logical_and(local >= 0.0, local < 256.0)
            sendhot[t, part * 256 : (part + 1) * 256, :] = one_hot_rows(
                jnp.where(inside, local, -1.0), iota_ref[...]
            )

    def lend(phase, table):
        own = jnp.concatenate([table[2 + t] for t in range(8)], axis=1)
        for side in range(2):
            lent = dot(own, side_by_side(sendhot[2 * side], sendhot[2 * side + 1])).astype(BF16)
            for t in range(2):
                sendh[phase, 2 * side + t] = lent[:, tile_of(t)]

    lend(0, t1)
    back_sq, fore_sq = reduce_wait(0, 2)
    back_len = jnp.sqrt(back_sq + 1e-06)
    fore_len = jnp.sqrt(fore_sq + 1e-06)
    tangent = (pos[...] - band[0]) / back_len + (band[1] - pos[...]) / fore_len
    tang[...] = tangent
    for copy in h_copies(0, t1):
        copy.start()
    reduce_start(1, (total(jnp.sum(tangent * tangent, axis=0)),))

    def gathered(table, layer, tile, pair):
        s = 2 * pair
        hot = side_by_side(onehot[tile, s], onehot[tile, s + 1])
        fars = [
            dot(side_by_side(table[tile + 2 * part], table[tile + 2 * part + 1]), hot)
            for part in range(2)
        ]
        rows = pl.multiple_of(s * RAD, 2 * RAD)
        both = hid[layer, tile, pl.ds(rows, 2 * RAD), :]
        field = dot(rad_t[layer + 1], side_by_side(both[:RAD], both[RAD:]))
        far = []
        for side in range(2):
            index = jnp.broadcast_to(rel[tile, pl.ds(s + side, 1), :], (8, LANES))
            low = index & 127
            second = (index >> 8) == 1
            third = (index >> 8) == 2
            pieces = []
            for g in range(C // 8):
                rows8 = slice(8 * g, 8 * g + 8)
                value = jnp.where(second, fars[1][rows8, tile_of(side)], fars[0][rows8, tile_of(side)])
                pieces.append(jnp.where(third, lane_gather(last_ref[rows8, :], low), value))
            far.append(jnp.concatenate(pieces, axis=0))
        return far, field

    def tile_loop(table, phase, body):
        def step(i, _):
            tile = lax.rem(i + 2, TILES)

            @pl.when(i == 4)
            def _():
                for copy in h_copies(phase, table):
                    copy.wait()

            last_ref[...] = table[tile + 4].astype(F32)
            body(tile)
            return 0

        lax.fori_loop(0, TILES, step, 0)

    def second_tile(tile):
        def pair(p, acc):
            far, field = gathered(t1, 0, tile, p)
            return acc + (far[0] * field[:, tile_of(0)] + far[1] * field[:, tile_of(1)])

        summed = lax.fori_loop(0, FAN // 2, pair, jnp.zeros((C, LANES), F32), unroll=UNROLL)
        scaled_ref[tile] = (summed / math.sqrt(FAN)).astype(BF16)

    tile_loop(t1, 0, second_tile)
    for t in range(0, TILES, 2):
        half = dot(mix_t[1], side_by_side(scaled_ref[t], scaled_ref[t + 1])) * 0.5
        update = half + half * jnp.tanh(half)
        for side in range(2):
            at = t + side + 2
            t2[at] = (t1[at].astype(F32) + update[:, tile_of(side)]).astype(BF16)
    lend(1, t2)
    (tau_sq,) = reduce_wait(1, 1)
    for copy in h_copies(1, t2):
        copy.start()

    def force_tile(tile):
        at = pl.multiple_of(tile * LANES, LANES)
        own_ref[...] = t2[tile + 2].astype(F32)

        def pair(p, acc):
            far, field = gathered(t2, 1, tile, p)
            for side in range(2):
                work = far[side] * field[:, tile_of(side)] * own_ref[...]
                strip = jnp.sum(work.reshape(C // 8, 8, LANES), axis=0)
                acc = tuple(
                    acc[comp] + strip * delta[comp, tile, pl.ds(2 * p + side, 1), :]
                    for comp in range(3)
                )
            return acc

        zero = jnp.zeros((8, LANES), F32)
        parts = lax.fori_loop(0, FAN // 2, pair, (zero, zero, zero), unroll=UNROLL)
        for comp in range(3):
            force[comp, :, pl.ds(at, LANES)] = jnp.sum(parts[comp], axis=0, keepdims=True) * (
                1.0 / math.sqrt(C)
            )

    tile_loop(t2, 1, force_tile)

    own = jnp.concatenate([t2[2 + t] for t in range(8)], axis=1)
    per_atom = dot(jnp.broadcast_to(w_energy[...], (16, C)), own)[0:1, :]
    for k in range(SPECIES):
        per_atom = per_atom + jnp.where(species[...] == k, ref_energy[k], 0.0)
    pull = force[...]
    tangent = tang[...]
    reduce_start(
        2,
        (
            jnp.sum(per_atom, axis=1, keepdims=True),
            total(jnp.sum(pull * tangent, axis=0)),
        ),
    )
    energy, along = reduce_wait(2, 2)
    energy_out[...] = energy / (ATOMS * n_atom)
    proj = along / tau_sq
    interior = (
        pull - proj * tangent + SPRING * (fore_len - back_len) / jnp.sqrt(tau_sq) * tangent
    )
    climbing = pull - 2.0 * proj * tangent
    is_end = jnp.logical_or(img == 0, img == n_img - 1)
    band_force = jnp.where(climb[...] == 1, climbing, interior)
    out[...] = jnp.where(is_end, pull, band_force)


def on_device(
    n_img,
    n_atom,
    positions,
    species,
    counts,
    neighbours,
    send_list,
    climb,
    embed,
    ref_energy,
    rad_in,
    rad_out,
    mixing,
    w_energy,
):
    vmem = pl.BlockSpec(memory_space=pltpu.VMEM)
    smem = pl.BlockSpec(memory_space=pltpu.SMEM)
    dma = pltpu.SemaphoreType.DMA
    result, energy = pl.pallas_call(
        functools.partial(kernel, n_img, n_atom),
        out_shape=(
            jax.ShapeDtypeStruct((3, 1, ATOMS), F32),
            jax.ShapeDtypeStruct((1, 1), F32),
        ),
        in_specs=[vmem, vmem, vmem, vmem, vmem, vmem, vmem, smem, vmem, vmem, vmem, vmem],
        out_specs=(vmem, vmem),
        scratch_shapes=[
            pltpu.VMEM((8, TABLE), F32),
            pltpu.VMEM((8, 2 * HALO), F32),
            pltpu.VMEM((2, 3, 1, ATOMS), F32),
            pltpu.VMEM((12, C, LANES), BF16),
            pltpu.VMEM((12, C, LANES), BF16),
            pltpu.VMEM((2, 4, C, LANES), BF16),
            pltpu.VMEM((TILES, FAN, 256, LANES), BF16),
            pltpu.VMEM((4, ATOMS, LANES), BF16),
            pltpu.VMEM((256, LANES), BF16),
            pltpu.VMEM((2, TILES, FAN * RAD, LANES), BF16),
            pltpu.VMEM((2, FAN * 256, LANES), BF16),
            pltpu.VMEM((FAN * 192, C), BF16),
            pltpu.VMEM((C, FAN * 256), BF16),
            pltpu.VMEM((3, C, RAD), BF16),
            pltpu.VMEM((2, C, C), BF16),
            pltpu.VMEM((C, C), BF16),
            pltpu.VMEM((2, C, LANES), BF16),
            pltpu.VMEM((2, SPECIES, FAN, LANES), F32),
            pltpu.VMEM((3, TILES, FAN, LANES), F32),
            pltpu.VMEM((TILES, FAN, LANES), I32),
            pltpu.VMEM((TILES, C, LANES), BF16),
            pltpu.VMEM((C, LANES), F32),
            pltpu.VMEM((C, LANES), F32),
            pltpu.VMEM((3, 1, ATOMS), F32),
            pltpu.VMEM((3, 1, ATOMS), F32),
            pltpu.VMEM((3, n_atom, 1, LANES), F32),
            dma((2,)),
            dma((2,)),
            dma((2,)),
            dma((2,)),
            dma((2, 2)),
            dma((2, 2)),
            dma((3,)),
            dma((3,)),
        ],
        compiler_params=pltpu.CompilerParams(
            collective_id=0, has_side_effects=True, vmem_limit_bytes=60 * 1024 * 1024
        ),
        name="band_step",
    )(
        positions.transpose(1, 0, 2),
        species.reshape(1, ATOMS),
        counts.reshape(1, ATOMS),
        neighbours,
        send_list.reshape(1, 2 * HALO),
        climb.reshape(1, 1),
        embed,
        ref_energy,
        rad_in,
        rad_out,
        mixing,
        w_energy.reshape(1, C),
    )
    return result.transpose(1, 0, 2), energy.reshape(1)


def solution(mesh):
    return jax.shard_map(
        functools.partial(on_device, mesh.shape["img"], mesh.shape["atom"]),
        mesh=mesh,
        in_specs=(
            P("img", None, "atom"),
            P("atom"),
            P("atom"),
            P(None, "atom"),
            P("atom"),
            P("img"),
            P(),
            P(),
            P(),
            P(),
            P(),
            P(),
        ),
        out_specs=(P("img", None, "atom"), P("img")),
        check_vma=False,
    )
```

```python
import functools
import math

import jax
import jax.numpy as jnp
from jax import lax
from jax.experimental import pallas as pl
from jax.experimental.pallas import tpu as pltpu
from jax.sharding import PartitionSpec as P

F32 = jnp.float32
BF16 = jnp.bfloat16
I32 = jnp.int32
MESH = pl.DeviceIdType.MESH

SPRING = 5.0
C = 128
RAD = 64
NB = 8
SPECIES = 4
FAN = 16
HALO = 256
ATOMS = 1024
BLK = 256
BLOCKS = ATOMS // BLK
LANES = 128
WIN = LANES + 2 * HALO
TILES = ATOMS // LANES
TABLE = ATOMS + 2 * HALO
UNROLL = 8
HID_UNROLL = 4
FAR_AWAY = 1.0e4


def lane_gather(source, index):
    return jnp.take_along_axis(source, index, axis=1, mode="promise_in_bounds")


def dot(a, b):
    return jnp.dot(a, b, preferred_element_type=F32)


def total(x):
    return jnp.sum(jnp.sum(x, axis=0, keepdims=True), axis=1, keepdims=True)


def one_hot_rows(local, iota):
    local = jnp.broadcast_to(local, (16, LANES)).astype(BF16)
    local = jnp.concatenate([local] * 16, axis=0)
    return jnp.where(local == iota, jnp.ones_like(iota), jnp.zeros_like(iota))


def side_by_side(left, right):
    return jnp.concatenate([left, right], axis=1)


def tile_of(lane):
    return slice(lane * LANES, (lane + 1) * LANES)


def kernel(
    n_img,
    n_atom,
    pos,
    species,
    counts,
    neighbours,
    send_list,
    climb,
    embed,
    ref_energy,
    rad_in,
    rad_out,
    mixing,
    w_energy,
    out,
    energy_out,
    ptab,
    sendpos,
    band,
    t1,
    t2,
    sendh,
    sendhot,
    iota_ref,
    hid,
    w_hid,
    rad_t,
    mix_t,
    emb_t,
    basis,
    kind,
    delta,
    rel,
    scaled_ref,
    last_ref,
    own_ref,
    force,
    tang,
    rbuf,
    pos_send,
    pos_recv,
    img_send,
    img_recv,
    h_send,
    h_recv,
    r_send,
    r_recv,
):
    img = lax.axis_index("img")
    me = lax.axis_index("atom")

    def ring(index, step, size):
        moved = index + step
        return jnp.where(moved >= size, moved - size, moved)

    up = ring(me, 1, n_atom)
    down = ring(me, n_atom - 1, n_atom)
    img_up = ring(img, 1, n_img)
    img_down = ring(img, n_img - 1, n_img)

    barrier = pltpu.get_barrier_semaphore()
    for d in range(1, n_atom):
        pl.semaphore_signal(
            barrier, inc=1, device_id=(img, ring(me, d, n_atom)), device_id_type=MESH
        )
    for other in (img_up, img_down):
        pl.semaphore_signal(barrier, inc=1, device_id=(other, me), device_id_type=MESH)

    own_cols = slice(HALO, HALO + ATOMS)
    for comp in range(3):
        ptab[comp : comp + 1, own_cols] = pos[comp]
    ptab[3:4, own_cols] = species[...].astype(F32)
    ptab[4:8, own_cols] = jnp.zeros((4, ATOMS), F32)
    for t in range(4):
        index = jnp.broadcast_to(send_list[:, tile_of(t)], (8, LANES))
        low = index & 127
        high = index >> 7
        got = jnp.zeros((8, LANES), F32)
        for w in range(ATOMS // LANES):
            source = ptab[:, HALO + w * LANES : HALO + (w + 1) * LANES]
            got = jnp.where(high == w, lane_gather(source, low), got)
        sendpos[:, tile_of(t)] = got

    iota_ref[...] = lax.broadcasted_iota(I32, (256, LANES), 0).astype(F32).astype(BF16)
    for layer in range(3):
        rad_t[layer] = rad_out[layer].astype(F32).T.astype(BF16)
    for layer in range(2):
        mix_t[layer] = mixing[layer].astype(F32).T.astype(BF16)
    emb = embed[...].astype(F32)
    emb_rows = jnp.concatenate([emb, jnp.zeros((C - SPECIES, C), F32)], axis=0)
    emb_t[...] = emb_rows.T.astype(BF16)
    lane = lax.broadcasted_iota(I32, (NB, C), 1)
    spread = (lane // FAN == lax.broadcasted_iota(I32, (NB, C), 0)).astype(F32).astype(BF16)
    lane64 = lax.broadcasted_iota(I32, (RAD, C), 1) % FAN
    for layer in range(3):
        wide = lax.dot_general(
            rad_in[layer], spread, (((0,), (0,)), ((), ())), preferred_element_type=F32
        )
        wide = wide * 0.5
        for s in range(FAN):
            start = s * 192 + layer * RAD
            w_hid[start : start + RAD, :] = jnp.where(lane64 == s, wide, 0.0).astype(BF16)

    def copy_to(source, target, send, recv, device):
        return pltpu.make_async_remote_copy(
            src_ref=source,
            dst_ref=target,
            send_sem=send,
            recv_sem=recv,
            device_id=device,
            device_id_type=MESH,
        )

    def pos_copies():
        low, high = slice(0, HALO), slice(HALO + ATOMS, TABLE)
        return (
            copy_to(
                sendpos.at[:, 0:HALO], ptab.at[:, high], pos_send.at[0], pos_recv.at[0], (img, down)
            ),
            copy_to(
                sendpos.at[:, HALO : 2 * HALO],
                ptab.at[:, low],
                pos_send.at[1],
                pos_recv.at[1],
                (img, up),
            ),
        )

    def img_copies():
        return (
            copy_to(pos, band.at[0], img_send.at[0], img_recv.at[0], (img_up, me)),
            copy_to(pos, band.at[1], img_send.at[1], img_recv.at[1], (img_down, me)),
        )

    def h_copies(phase, table):
        return (
            copy_to(
                sendh.at[phase, 0:2],
                table.at[10:12],
                h_send.at[phase, 0],
                h_recv.at[phase, 0],
                (img, down),
            ),
            copy_to(
                sendh.at[phase, 2:4],
                table.at[0:2],
                h_send.at[phase, 1],
                h_recv.at[phase, 1],
                (img, up),
            ),
        )

    lane_row = lax.broadcasted_iota(I32, (1, LANES), 1)

    def reduce_start(phase, values):
        message = jnp.zeros((1, LANES), F32)
        for n, value in enumerate(values):
            message = jnp.where(lane_row == n, value, message)
        rbuf[phase, me] = message
        for d in range(1, n_atom):
            copy_to(
                rbuf.at[phase, me],
                rbuf.at[phase, me],
                r_send.at[phase],
                r_recv.at[phase],
                (img, ring(me, d, n_atom)),
            ).start()

    def reduce_wait(phase, number):
        others = rbuf.at[phase, 0 : n_atom - 1]
        arrived = copy_to(others, others, r_send.at[phase], r_recv.at[phase], (img, up))
        arrived.wait_send()
        arrived.wait_recv()
        summed = jnp.sum(rbuf[phase], axis=0)
        return [
            jnp.sum(jnp.where(lane_row == n, summed, 0.0), axis=1, keepdims=True)
            for n in range(number)
        ]

    def first_block(i, _):
        block = lax.rem(i + 1, BLOCKS)
        start = pl.multiple_of(block * BLK, BLK)

        @pl.when(i == 1)
        def _():
            pl.semaphore_wait(barrier, n_atom + 1)
            for copy in pos_copies() + img_copies():
                copy.start()

        @pl.when(i == 2)
        def _():
            for copy in pos_copies() + img_copies():
                copy.wait()
            behind = pos[...] - band[0]
            ahead = band[1] - pos[...]
            reduce_start(
                0, (total(jnp.sum(behind * behind, axis=0)), total(jnp.sum(ahead * ahead, axis=0)))
            )

        for t in range(BLK // LANES):
            at = pl.multiple_of(start + t * LANES, LANES)
            tile = block * 2 + t
            offset = neighbours[:, pl.ds(at, LANES)] - at
            rel[tile] = offset
            low = offset & 127
            high = offset >> 7
            got = [None] * 4
            for w in range(WIN // LANES):
                here = high == w
                for comp in range(4):
                    source = jnp.broadcast_to(
                        ptab[comp : comp + 1, pl.ds(pl.multiple_of(at + w * LANES, LANES), LANES)],
                        (FAN, LANES),
                    )
                    value = lane_gather(source, low)
                    got[comp] = value if w == 0 else jnp.where(here, value, got[comp])
            slots = lax.broadcasted_iota(I32, (FAN, LANES), 0)
            live = slots < counts[:, pl.ds(at, LANES)]
            dist = jnp.zeros((FAN, LANES), F32)
            for comp in range(3):
                diff = got[comp] - pos[comp, :, pl.ds(at, LANES)]
                delta[comp, tile] = diff
                dist = dist + diff * diff
            dist = jnp.where(live, dist, FAR_AWAY)
            for k in range(NB):
                shifted = dist - 2.0 * k
                basis[t, k * FAN : (k + 1) * FAN, :] = jnp.exp(-(shifted * shifted) / 8.0).astype(
                    BF16
                )
            kind[tile] = got[3].astype(I32)

        def slot(s, _):
            rows = pl.multiple_of(s * 192, 192)
            half = dot(w_hid[pl.ds(rows, 192), :], side_by_side(basis[0], basis[1]))
            unit = (half + half * jnp.tanh(half)).astype(BF16)
            for t in range(BLK // LANES):
                hid[block * 2 + t, pl.ds(rows, 192), :] = unit[:, tile_of(t)]
            return 0

        lax.fori_loop(0, FAN, slot, 0, unroll=HID_UNROLL)
        return 0

    lax.fori_loop(0, BLOCKS, first_block, 0)

    def radial(layer, tile, pair):
        sides = [
            hid[tile, pl.ds(pl.multiple_of((2 * pair + n) * 192 + layer * RAD, RAD), RAD), :]
            for n in range(2)
        ]
        return dot(rad_t[layer], side_by_side(*sides))

    def update_of(layer, t):
        half = dot(mix_t[layer], side_by_side(scaled_ref[t], scaled_ref[t + 1])) * 0.5
        return half + half * jnp.tanh(half)

    last_ref[...] = emb_t[...].astype(F32)

    def first_tile(tile, _):
        def pair(p, acc):
            field = radial(0, tile, p)
            for side in range(2):
                index = jnp.broadcast_to(kind[tile, pl.ds(2 * p + side, 1), :], (8, LANES))
                far = [lane_gather(last_ref[8 * g : 8 * g + 8, :], index) for g in range(C // 8)]
                acc = acc + jnp.concatenate(far, axis=0) * field[:, tile_of(side)]
            return acc

        summed = lax.fori_loop(0, FAN // 2, pair, jnp.zeros((C, LANES), F32), unroll=UNROLL)
        scaled_ref[tile] = (summed / math.sqrt(FAN)).astype(BF16)
        return 0

    lax.fori_loop(0, TILES, first_tile, 0)
    for t in range(0, TILES, 2):
        kinds = jnp.broadcast_to(species[:, t * LANES : (t + 2) * LANES], (16, 2 * LANES))
        own_hot = (kinds == lax.broadcasted_iota(I32, kinds.shape, 0)).astype(F32).astype(BF16)
        h1 = (dot(emb_t[:, :16], own_hot) + update_of(0, t)).astype(BF16)
        for side in range(2):
            t1[t + side + 2] = h1[:, tile_of(side)]

    for t in range(2 * HALO // LANES):
        index = send_list[:, tile_of(t)].astype(F32)
        for part in range(ATOMS // 256):
            local = index - 256.0 * part
            inside = jnp.logical_and(local >= 0.0, local < 256.0)
            sendhot[t, part * 256 : (part + 1) * 256, :] = one_hot_rows(
                jnp.where(inside, local, -1.0), iota_ref[...]
            )

    def lend(phase, table):
        own = jnp.concatenate([table[2 + t] for t in range(8)], axis=1)
        for side in range(2):
            lent = dot(own, side_by_side(sendhot[2 * side], sendhot[2 * side + 1])).astype(BF16)
            for t in range(2):
                sendh[phase, 2 * side + t] = lent[:, tile_of(t)]

    lend(0, t1)
    back_sq, fore_sq = reduce_wait(0, 2)
    back_len = jnp.sqrt(back_sq + 1e-06)
    fore_len = jnp.sqrt(fore_sq + 1e-06)
    tangent = (pos[...] - band[0]) / back_len + (band[1] - pos[...]) / fore_len
    tang[...] = tangent
    for copy in h_copies(0, t1):
        copy.start()
    reduce_start(1, (total(jnp.sum(tangent * tangent, axis=0)),))

    def gathered(table, layer, tile, pair):
        hot = side_by_side(
            *[
                one_hot_rows((rel[tile, pl.ds(2 * pair + n, 1), :] & 255).astype(F32), iota_ref[...])
                for n in range(2)
            ]
        )
        near = jnp.concatenate(
            [side_by_side(table[tile + 2 * n], table[tile + 2 * n + 1]) for n in range(2)], axis=0
        )
        both = dot(near, hot)
        fars = both[:C], both[C:]
        field = radial(layer + 1, tile, pair)
        far = []
        for side in range(2):
            index = jnp.broadcast_to(rel[tile, pl.ds(2 * pair + side, 1), :], (8, LANES))
            low = index & 127
            second = (index >> 8) == 1
            third = (index >> 8) == 2
            pieces = []
            for g in range(C // 8):
                rows8 = slice(8 * g, 8 * g + 8)
                value = jnp.where(second, fars[1][rows8, tile_of(side)], fars[0][rows8, tile_of(side)])
                pieces.append(jnp.where(third, lane_gather(last_ref[rows8, :], low), value))
            far.append(jnp.concatenate(pieces, axis=0))
        return far, field

    def tile_loop(table, phase, body):
        def step(i, _):
            tile = lax.rem(i + 2, TILES)

            @pl.when(i == 4)
            def _():
                for copy in h_copies(phase, table):
                    copy.wait()

            last_ref[...] = table[tile + 4].astype(F32)
            body(tile)
            return 0

        lax.fori_loop(0, TILES, step, 0)

    def second_tile(tile):
        def pair(p, acc):
            far, field = gathered(t1, 0, tile, p)
            return acc + (far[0] * field[:, tile_of(0)] + far[1] * field[:, tile_of(1)])

        summed = lax.fori_loop(0, FAN // 2, pair, jnp.zeros((C, LANES), F32), unroll=UNROLL)
        scaled_ref[tile] = (summed / math.sqrt(FAN)).astype(BF16)

    tile_loop(t1, 0, second_tile)
    for t in range(0, TILES, 2):
        update = update_of(1, t)
        for side in range(2):
            at = t + side + 2
            t2[at] = (t1[at].astype(F32) + update[:, tile_of(side)]).astype(BF16)
    lend(1, t2)
    (tau_sq,) = reduce_wait(1, 1)
    for copy in h_copies(1, t2):
        copy.start()

    def force_tile(tile):
        at = pl.multiple_of(tile * LANES, LANES)
        own_ref[...] = t2[tile + 2].astype(F32)

        def pair(p, acc):
            far, field = gathered(t2, 1, tile, p)
            for side in range(2):
                work = far[side] * field[:, tile_of(side)] * own_ref[...]
                strip = jnp.sum(work.reshape(C // 8, 8, LANES), axis=0)
                acc = tuple(
                    acc[comp] + strip * delta[comp, tile, pl.ds(2 * p + side, 1), :]
                    for comp in range(3)
                )
            return acc

        zero = jnp.zeros((8, LANES), F32)
        parts = lax.fori_loop(0, FAN // 2, pair, (zero, zero, zero), unroll=UNROLL)
        for comp in range(3):
            force[comp, :, pl.ds(at, LANES)] = jnp.sum(parts[comp], axis=0, keepdims=True) * (
                1.0 / math.sqrt(C)
            )

    tile_loop(t2, 1, force_tile)

    own = jnp.concatenate([t2[2 + t] for t in range(8)], axis=1)
    per_atom = dot(jnp.broadcast_to(w_energy[...], (16, C)), own)[0:1, :]
    for k in range(SPECIES):
        per_atom = per_atom + jnp.where(species[...] == k, ref_energy[k], 0.0)
    pull = force[...]
    tangent = tang[...]
    reduce_start(
        2,
        (
            jnp.sum(per_atom, axis=1, keepdims=True),
            total(jnp.sum(pull * tangent, axis=0)),
        ),
    )
    energy, along = reduce_wait(2, 2)
    energy_out[...] = energy / (ATOMS * n_atom)
    proj = along / tau_sq
    interior = (
        pull - proj * tangent + SPRING * (fore_len - back_len) / jnp.sqrt(tau_sq) * tangent
    )
    climbing = pull - 2.0 * proj * tangent
    is_end = jnp.logical_or(img == 0, img == n_img - 1)
    band_force = jnp.where(climb[...] == 1, climbing, interior)
    out[...] = jnp.where(is_end, pull, band_force)


def on_device(
    n_img,
    n_atom,
    positions,
    species,
    counts,
    neighbours,
    send_list,
    climb,
    embed,
    ref_energy,
    rad_in,
    rad_out,
    mixing,
    w_energy,
):
    vmem = pl.BlockSpec(memory_space=pltpu.VMEM)
    smem = pl.BlockSpec(memory_space=pltpu.SMEM)
    dma = pltpu.SemaphoreType.DMA
    result, energy = pl.pallas_call(
        functools.partial(kernel, n_img, n_atom),
        out_shape=(
            jax.ShapeDtypeStruct((3, 1, ATOMS), F32),
            jax.ShapeDtypeStruct((1, 1), F32),
        ),
        in_specs=[vmem, vmem, vmem, vmem, vmem, vmem, vmem, smem, vmem, vmem, vmem, vmem],
        out_specs=(vmem, vmem),
        scratch_shapes=[
            pltpu.VMEM((8, TABLE), F32),
            pltpu.VMEM((8, 2 * HALO), F32),
            pltpu.VMEM((2, 3, 1, ATOMS), F32),
            pltpu.VMEM((12, C, LANES), BF16),
            pltpu.VMEM((12, C, LANES), BF16),
            pltpu.VMEM((2, 4, C, LANES), BF16),
            pltpu.VMEM((4, ATOMS, LANES), BF16),
            pltpu.VMEM((256, LANES), BF16),
            pltpu.VMEM((TILES, FAN * 192, LANES), BF16),
            pltpu.VMEM((FAN * 192, C), BF16),
            pltpu.VMEM((3, C, RAD), BF16),
            pltpu.VMEM((2, C, C), BF16),
            pltpu.VMEM((C, C), BF16),
            pltpu.VMEM((2, C, LANES), BF16),
            pltpu.VMEM((TILES, FAN, LANES), I32),
            pltpu.VMEM((3, TILES, FAN, LANES), F32),
            pltpu.VMEM((TILES, FAN, LANES), I32),
            pltpu.VMEM((TILES, C, LANES), BF16),
            pltpu.VMEM((C, LANES), F32),
            pltpu.VMEM((C, LANES), F32),
            pltpu.VMEM((3, 1, ATOMS), F32),
            pltpu.VMEM((3, 1, ATOMS), F32),
            pltpu.VMEM((3, n_atom, 1, LANES), F32),
            dma((2,)),
            dma((2,)),
            dma((2,)),
            dma((2,)),
            dma((2, 2)),
            dma((2, 2)),
            dma((3,)),
            dma((3,)),
        ],
        compiler_params=pltpu.CompilerParams(
            collective_id=0, has_side_effects=True, vmem_limit_bytes=60 * 1024 * 1024
        ),
        name="band_step",
    )(
        positions.transpose(1, 0, 2),
        species.reshape(1, ATOMS),
        counts.reshape(1, ATOMS),
        neighbours,
        send_list.reshape(1, 2 * HALO),
        climb.reshape(1, 1),
        embed,
        ref_energy,
        rad_in,
        rad_out,
        mixing,
        w_energy.reshape(1, C),
    )
    return result.transpose(1, 0, 2), energy.reshape(1)


def solution(mesh):
    return jax.shard_map(
        functools.partial(on_device, mesh.shape["img"], mesh.shape["atom"]),
        mesh=mesh,
        in_specs=(
            P("img", None, "atom"),
            P("atom"),
            P("atom"),
            P(None, "atom"),
            P("atom"),
            P("img"),
            P(),
            P(),
            P(),
            P(),
            P(),
            P(),
        ),
        out_specs=(P("img", None, "atom"), P("img")),
        check_vma=False,
    )
```

```python
import functools
import math

import jax
import jax.numpy as jnp
from jax import lax
from jax.experimental import pallas as pl
from jax.experimental.pallas import tpu as pltpu
from jax.sharding import PartitionSpec as P

F32 = jnp.float32
BF16 = jnp.bfloat16
I32 = jnp.int32
MESH = pl.DeviceIdType.MESH

SPRING = 5.0
C = 128
RAD = 64
NB = 8
SPECIES = 4
FAN = 16
HALO = 256
ATOMS = 1024
BLK = 256
BLOCKS = ATOMS // BLK
LANES = 128
WIN = LANES + 2 * HALO
TILES = ATOMS // LANES
TABLE = ATOMS + 2 * HALO
UNROLL = 8
HID_UNROLL = 16
FAR_AWAY = 1.0e4


def lane_gather(source, index):
    return jnp.take_along_axis(source, index, axis=1, mode="promise_in_bounds")


def dot(a, b):
    return jnp.dot(a, b, preferred_element_type=F32)


def total(x):
    return jnp.sum(jnp.sum(x, axis=0, keepdims=True), axis=1, keepdims=True)


def one_hot_rows(local, iota):
    local = jnp.broadcast_to(local, (16, LANES)).astype(BF16)
    local = jnp.concatenate([local] * 16, axis=0)
    return jnp.where(local == iota, jnp.ones_like(iota), jnp.zeros_like(iota))


def side_by_side(left, right):
    return jnp.concatenate([left, right], axis=1)


def tile_of(lane):
    return slice(lane * LANES, (lane + 1) * LANES)


def kernel(
    n_img,
    n_atom,
    pos,
    species,
    counts,
    neighbours,
    send_list,
    climb,
    embed,
    ref_energy,
    rad_in,
    rad_out,
    mixing,
    w_energy,
    out,
    energy_out,
    ptab,
    sendpos,
    band,
    t1,
    t2,
    sendh,
    sendhot,
    iota_ref,
    hid,
    w_hid,
    rad_t,
    mix_t,
    emb_t,
    basis,
    kind,
    delta,
    rel,
    scaled_ref,
    last_ref,
    own_ref,
    force,
    tang,
    rbuf,
    pos_send,
    pos_recv,
    img_send,
    img_recv,
    h_send,
    h_recv,
    r_send,
    r_recv,
):
    img = lax.axis_index("img")
    me = lax.axis_index("atom")

    def ring(index, step, size):
        moved = index + step
        return jnp.where(moved >= size, moved - size, moved)

    up = ring(me, 1, n_atom)
    down = ring(me, n_atom - 1, n_atom)
    img_up = ring(img, 1, n_img)
    img_down = ring(img, n_img - 1, n_img)

    barrier = pltpu.get_barrier_semaphore()
    for d in range(1, n_atom):
        pl.semaphore_signal(
            barrier, inc=1, device_id=(img, ring(me, d, n_atom)), device_id_type=MESH
        )
    for other in (img_up, img_down):
        pl.semaphore_signal(barrier, inc=1, device_id=(other, me), device_id_type=MESH)

    own_cols = slice(HALO, HALO + ATOMS)
    for comp in range(3):
        ptab[comp : comp + 1, own_cols] = pos[comp]
    ptab[3:4, own_cols] = species[...].astype(F32)
    ptab[4:8, own_cols] = jnp.zeros((4, ATOMS), F32)
    for t in range(4):
        index = jnp.broadcast_to(send_list[:, tile_of(t)], (8, LANES))
        low = index & 127
        high = index >> 7
        got = jnp.zeros((8, LANES), F32)
        for w in range(ATOMS // LANES):
            source = ptab[:, HALO + w * LANES : HALO + (w + 1) * LANES]
            got = jnp.where(high == w, lane_gather(source, low), got)
        sendpos[:, tile_of(t)] = got

    iota_ref[...] = lax.broadcasted_iota(I32, (256, LANES), 0).astype(F32).astype(BF16)
    for layer in range(3):
        rad_t[layer] = rad_out[layer].astype(F32).T.astype(BF16)
    for layer in range(2):
        mix_t[layer] = mixing[layer].astype(F32).T.astype(BF16)
    emb = embed[...].astype(F32)
    emb_rows = jnp.concatenate([emb, jnp.zeros((C - SPECIES, C), F32)], axis=0)
    emb_t[...] = emb_rows.T.astype(BF16)
    lane = lax.broadcasted_iota(I32, (NB, C), 1)
    spread = (lane // FAN == lax.broadcasted_iota(I32, (NB, C), 0)).astype(F32).astype(BF16)
    lane64 = lax.broadcasted_iota(I32, (RAD, C), 1) % FAN
    for layer in range(3):
        wide = lax.dot_general(
            rad_in[layer], spread, (((0,), (0,)), ((), ())), preferred_element_type=F32
        )
        wide = wide * 0.5
        for s in range(FAN):
            start = s * 192 + layer * RAD
            w_hid[start : start + RAD, :] = jnp.where(lane64 == s, wide, 0.0).astype(BF16)

    def copy_to(source, target, send, recv, device):
        return pltpu.make_async_remote_copy(
            src_ref=source,
            dst_ref=target,
            send_sem=send,
            recv_sem=recv,
            device_id=device,
            device_id_type=MESH,
        )

    def pos_copies():
        low, high = slice(0, HALO), slice(HALO + ATOMS, TABLE)
        return (
            copy_to(
                sendpos.at[:, 0:HALO], ptab.at[:, high], pos_send.at[0], pos_recv.at[0], (img, down)
            ),
            copy_to(
                sendpos.at[:, HALO : 2 * HALO],
                ptab.at[:, low],
                pos_send.at[1],
                pos_recv.at[1],
                (img, up),
            ),
        )

    def img_copies():
        return (
            copy_to(pos, band.at[0], img_send.at[0], img_recv.at[0], (img_up, me)),
            copy_to(pos, band.at[1], img_send.at[1], img_recv.at[1], (img_down, me)),
        )

    def h_copies(phase, table):
        return (
            copy_to(
                sendh.at[phase, 0:2],
                table.at[10:12],
                h_send.at[phase, 0],
                h_recv.at[phase, 0],
                (img, down),
            ),
            copy_to(
                sendh.at[phase, 2:4],
                table.at[0:2],
                h_send.at[phase, 1],
                h_recv.at[phase, 1],
                (img, up),
            ),
        )

    lane_row = lax.broadcasted_iota(I32, (1, LANES), 1)

    def reduce_start(phase, values):
        message = jnp.zeros((1, LANES), F32)
        for n, value in enumerate(values):
            message = jnp.where(lane_row == n, value, message)
        rbuf[phase, me] = message
        for d in range(1, n_atom):
            copy_to(
                rbuf.at[phase, me],
                rbuf.at[phase, me],
                r_send.at[phase],
                r_recv.at[phase],
                (img, ring(me, d, n_atom)),
            ).start()

    def reduce_wait(phase, number):
        others = rbuf.at[phase, 0 : n_atom - 1]
        arrived = copy_to(others, others, r_send.at[phase], r_recv.at[phase], (img, up))
        arrived.wait_send()
        arrived.wait_recv()
        summed = jnp.sum(rbuf[phase], axis=0)
        return [
            jnp.sum(jnp.where(lane_row == n, summed, 0.0), axis=1, keepdims=True)
            for n in range(number)
        ]

    def radial(layer, tile, pair):
        sides = [
            hid[tile, pl.ds(pl.multiple_of((2 * pair + n) * 192 + layer * RAD, RAD), RAD), :]
            for n in range(2)
        ]
        return dot(rad_t[layer], side_by_side(*sides))

    def update_of(layer, t):
        half = dot(mix_t[layer], side_by_side(scaled_ref[t], scaled_ref[t + 1])) * 0.5
        return half + half * jnp.tanh(half)

    last_ref[...] = emb_t[...].astype(F32)

    def first_tile(tile, _):
        def pair(p, acc):
            field = radial(0, tile, p)
            for side in range(2):
                index = jnp.broadcast_to(kind[tile, pl.ds(2 * p + side, 1), :], (8, LANES))
                far = [lane_gather(last_ref[8 * g : 8 * g + 8, :], index) for g in range(C // 8)]
                acc = acc + jnp.concatenate(far, axis=0) * field[:, tile_of(side)]
            return acc

        summed = lax.fori_loop(0, FAN // 2, pair, jnp.zeros((C, LANES), F32), unroll=UNROLL)
        scaled_ref[tile] = (summed / math.sqrt(FAN)).astype(BF16)
        return 0

    def first_block(i, _):
        block = lax.rem(i + 1, BLOCKS)
        start = pl.multiple_of(block * BLK, BLK)

        @pl.when(i == 1)
        def _():
            pl.semaphore_wait(barrier, n_atom + 1)
            for copy in pos_copies() + img_copies():
                copy.start()

        @pl.when(i == 2)
        def _():
            for t in range(2 * HALO // LANES):
                index = send_list[:, tile_of(t)].astype(F32)
                for part in range(ATOMS // 256):
                    local = index - 256.0 * part
                    inside = jnp.logical_and(local >= 0.0, local < 256.0)
                    sendhot[t, part * 256 : (part + 1) * 256, :] = one_hot_rows(
                        jnp.where(inside, local, -1.0), iota_ref[...]
                    )

            lax.fori_loop(2, 6, first_tile, 0)
            for copy in pos_copies() + img_copies():
                copy.wait()
            behind = pos[...] - band[0]
            ahead = band[1] - pos[...]
            reduce_start(
                0, (total(jnp.sum(behind * behind, axis=0)), total(jnp.sum(ahead * ahead, axis=0)))
            )

        for t in range(BLK // LANES):
            at = pl.multiple_of(start + t * LANES, LANES)
            tile = block * 2 + t
            offset = neighbours[:, pl.ds(at, LANES)] - at
            rel[tile] = offset
            low = offset & 127
            high = offset >> 7
            got = [None] * 4
            for w in range(WIN // LANES):
                here = high == w
                for comp in range(4):
                    source = jnp.broadcast_to(
                        ptab[comp : comp + 1, pl.ds(pl.multiple_of(at + w * LANES, LANES), LANES)],
                        (FAN, LANES),
                    )
                    value = lane_gather(source, low)
                    got[comp] = value if w == 0 else jnp.where(here, value, got[comp])
            slots = lax.broadcasted_iota(I32, (FAN, LANES), 0)
            live = slots < counts[:, pl.ds(at, LANES)]
            dist = jnp.zeros((FAN, LANES), F32)
            for comp in range(3):
                diff = got[comp] - pos[comp, :, pl.ds(at, LANES)]
                delta[comp, tile] = diff
                dist = dist + diff * diff
            dist = jnp.where(live, dist, FAR_AWAY)
            for k in range(NB):
                shifted = dist - 2.0 * k
                basis[t, k * FAN : (k + 1) * FAN, :] = jnp.exp(-(shifted * shifted) / 8.0).astype(
                    BF16
                )
            kind[tile] = got[3].astype(I32)

        def slot(s, _):
            rows = pl.multiple_of(s * 192, 192)
            half = dot(w_hid[pl.ds(rows, 192), :], side_by_side(basis[0], basis[1]))
            unit = (half + half * jnp.tanh(half)).astype(BF16)
            for t in range(BLK // LANES):
                hid[block * 2 + t, pl.ds(rows, 192), :] = unit[:, tile_of(t)]
            return 0

        lax.fori_loop(0, FAN, slot, 0, unroll=HID_UNROLL)
        return 0

    lax.fori_loop(0, BLOCKS, first_block, 0)

    lax.fori_loop(6, 10, lambda i, _: first_tile(lax.rem(i, TILES), 0), 0)
    for t in range(0, TILES, 2):
        kinds = jnp.broadcast_to(species[:, t * LANES : (t + 2) * LANES], (16, 2 * LANES))
        own_hot = (kinds == lax.broadcasted_iota(I32, kinds.shape, 0)).astype(F32).astype(BF16)
        h1 = (dot(emb_t[:, :16], own_hot) + update_of(0, t)).astype(BF16)
        for side in range(2):
            t1[t + side + 2] = h1[:, tile_of(side)]

    def lend(phase, table):
        own = jnp.concatenate([table[2 + t] for t in range(8)], axis=1)
        for side in range(2):
            lent = dot(own, side_by_side(sendhot[2 * side], sendhot[2 * side + 1])).astype(BF16)
            for t in range(2):
                sendh[phase, 2 * side + t] = lent[:, tile_of(t)]

    lend(0, t1)
    for copy in h_copies(0, t1):
        copy.start()

    def gathered(table, layer, tile, pair):
        hot = side_by_side(
            *[
                one_hot_rows((rel[tile, pl.ds(2 * pair + n, 1), :] & 255).astype(F32), iota_ref[...])
                for n in range(2)
            ]
        )
        near = jnp.concatenate(
            [side_by_side(table[tile + 2 * n], table[tile + 2 * n + 1]) for n in range(2)], axis=0
        )
        both = dot(near, hot)
        fars = both[:C], both[C:]
        field = radial(layer + 1, tile, pair)
        far = []
        for side in range(2):
            index = jnp.broadcast_to(rel[tile, pl.ds(2 * pair + side, 1), :], (8, LANES))
            low = index & 127
            second = (index >> 8) == 1
            third = (index >> 8) == 2
            pieces = []
            for g in range(C // 8):
                rows8 = slice(8 * g, 8 * g + 8)
                value = jnp.where(second, fars[1][rows8, tile_of(side)], fars[0][rows8, tile_of(side)])
                pieces.append(jnp.where(third, lane_gather(last_ref[rows8, :], low), value))
            far.append(jnp.concatenate(pieces, axis=0))
        return far, field

    def tile_loop(table, phase, body):
        def step(i, _):
            tile = lax.rem(i + 2, TILES)

            @pl.when(i == 4)
            def _():
                for copy in h_copies(phase, table):
                    copy.wait()

            last_ref[...] = table[tile + 4].astype(F32)
            body(tile)
            return 0

        lax.fori_loop(0, TILES, step, 0)

    def second_tile(tile):
        def pair(p, acc):
            far, field = gathered(t1, 0, tile, p)
            return acc + (far[0] * field[:, tile_of(0)] + far[1] * field[:, tile_of(1)])

        summed = lax.fori_loop(0, FAN // 2, pair, jnp.zeros((C, LANES), F32), unroll=UNROLL)
        scaled_ref[tile] = (summed / math.sqrt(FAN)).astype(BF16)

    tile_loop(t1, 0, second_tile)
    for t in range(0, TILES, 2):
        update = update_of(1, t)
        for side in range(2):
            at = t + side + 2
            t2[at] = (t1[at].astype(F32) + update[:, tile_of(side)]).astype(BF16)
    lend(1, t2)
    for copy in h_copies(1, t2):
        copy.start()
    back_sq, fore_sq = reduce_wait(0, 2)
    back_len = jnp.sqrt(back_sq + 1e-06)
    fore_len = jnp.sqrt(fore_sq + 1e-06)
    tangent = (pos[...] - band[0]) / back_len + (band[1] - pos[...]) / fore_len
    tang[...] = tangent
    reduce_start(1, (total(jnp.sum(tangent * tangent, axis=0)),))

    def force_tile(tile):
        at = pl.multiple_of(tile * LANES, LANES)
        own_ref[...] = t2[tile + 2].astype(F32)

        def pair(p, acc):
            far, field = gathered(t2, 1, tile, p)
            for side in range(2):
                work = far[side] * field[:, tile_of(side)] * own_ref[...]
                strip = jnp.sum(work.reshape(C // 8, 8, LANES), axis=0)
                acc = tuple(
                    acc[comp] + strip * delta[comp, tile, pl.ds(2 * p + side, 1), :]
                    for comp in range(3)
                )
            return acc

        zero = jnp.zeros((8, LANES), F32)
        parts = lax.fori_loop(0, FAN // 2, pair, (zero, zero, zero), unroll=UNROLL)
        for comp in range(3):
            force[comp, :, pl.ds(at, LANES)] = jnp.sum(parts[comp], axis=0, keepdims=True) * (
                1.0 / math.sqrt(C)
            )

    tile_loop(t2, 1, force_tile)

    own = jnp.concatenate([t2[2 + t] for t in range(8)], axis=1)
    per_atom = dot(jnp.broadcast_to(w_energy[...], (16, C)), own)[0:1, :]
    for k in range(SPECIES):
        per_atom = per_atom + jnp.where(species[...] == k, ref_energy[k], 0.0)
    pull = force[...]
    tangent = tang[...]
    reduce_start(
        2,
        (
            jnp.sum(per_atom, axis=1, keepdims=True),
            total(jnp.sum(pull * tangent, axis=0)),
        ),
    )
    (tau_sq,) = reduce_wait(1, 1)
    energy, along = reduce_wait(2, 2)
    energy_out[...] = energy / (ATOMS * n_atom)
    proj = along / tau_sq
    interior = (
        pull - proj * tangent + SPRING * (fore_len - back_len) / jnp.sqrt(tau_sq) * tangent
    )
    climbing = pull - 2.0 * proj * tangent
    is_end = jnp.logical_or(img == 0, img == n_img - 1)
    band_force = jnp.where(climb[0] == 1, climbing, interior)
    out[...] = jnp.where(is_end, pull, band_force)


def finish(force, energy, force_out, energy_out):
    force_out[...] = force[...]
    energy_out[0] = energy[0, 0]


def on_device(
    n_img,
    n_atom,
    positions,
    species,
    counts,
    neighbours,
    send_list,
    climb,
    embed,
    ref_energy,
    rad_in,
    rad_out,
    mixing,
    w_energy,
):
    vmem = pl.BlockSpec(memory_space=pltpu.VMEM)
    smem = pl.BlockSpec(memory_space=pltpu.SMEM)
    dma = pltpu.SemaphoreType.DMA
    result, energy = pl.pallas_call(
        functools.partial(kernel, n_img, n_atom),
        out_shape=(
            jax.ShapeDtypeStruct((3, 1, ATOMS), F32),
            jax.ShapeDtypeStruct((1, 1), F32),
        ),
        in_specs=[vmem, vmem, vmem, vmem, vmem, smem, vmem, smem, vmem, vmem, vmem, vmem],
        out_specs=(vmem, vmem),
        scratch_shapes=[
            pltpu.VMEM((8, TABLE), F32),
            pltpu.VMEM((8, 2 * HALO), F32),
            pltpu.VMEM((2, 3, 1, ATOMS), F32),
            pltpu.VMEM((12, C, LANES), BF16),
            pltpu.VMEM((12, C, LANES), BF16),
            pltpu.VMEM((2, 4, C, LANES), BF16),
            pltpu.VMEM((4, ATOMS, LANES), BF16),
            pltpu.VMEM((256, LANES), BF16),
            pltpu.VMEM((TILES, FAN * 192, LANES), BF16),
            pltpu.VMEM((FAN * 192, C), BF16),
            pltpu.VMEM((3, C, RAD), BF16),
            pltpu.VMEM((2, C, C), BF16),
            pltpu.VMEM((C, C), BF16),
            pltpu.VMEM((2, C, LANES), BF16),
            pltpu.VMEM((TILES, FAN, LANES), I32),
            pltpu.VMEM((3, TILES, FAN, LANES), F32),
            pltpu.VMEM((TILES, FAN, LANES), I32),
            pltpu.VMEM((TILES, C, LANES), BF16),
            pltpu.VMEM((C, LANES), F32),
            pltpu.VMEM((C, LANES), F32),
            pltpu.VMEM((3, 1, ATOMS), F32),
            pltpu.VMEM((3, 1, ATOMS), F32),
            pltpu.VMEM((3, n_atom, 1, LANES), F32),
            dma((2,)),
            dma((2,)),
            dma((2,)),
            dma((2,)),
            dma((2, 2)),
            dma((2, 2)),
            dma((3,)),
            dma((3,)),
        ],
        compiler_params=pltpu.CompilerParams(
            collective_id=0, has_side_effects=True, vmem_limit_bytes=60 * 1024 * 1024
        ),
        name="band_step",
    )(
        positions.transpose(1, 0, 2),
        species.reshape(1, ATOMS),
        counts.reshape(1, ATOMS),
        neighbours,
        send_list.reshape(1, 2 * HALO),
        climb,
        embed,
        ref_energy,
        rad_in,
        rad_out,
        mixing,
        w_energy.reshape(1, C),
    )
    result, energy = pl.pallas_call(
        finish,
        out_shape=(
            jax.ShapeDtypeStruct((3, 1, ATOMS), F32),
            jax.ShapeDtypeStruct((1,), F32),
        ),
        in_specs=[vmem, smem],
        out_specs=(vmem, smem),
        name="finish",
    )(result, energy)
    return result.transpose(1, 0, 2), energy


def solution(mesh):
    return jax.shard_map(
        functools.partial(on_device, mesh.shape["img"], mesh.shape["atom"]),
        mesh=mesh,
        in_specs=(
            P("img", None, "atom"),
            P("atom"),
            P("atom"),
            P(None, "atom"),
            P("atom"),
            P("img"),
            P(),
            P(),
            P(),
            P(),
            P(),
            P(),
        ),
        out_specs=(P("img", None, "atom"), P("img")),
        check_vma=False,
    )
```

```python
import functools
import math

import jax
import jax.numpy as jnp
from jax import lax
from jax.experimental import pallas as pl
from jax.experimental.pallas import tpu as pltpu
from jax.sharding import PartitionSpec as P

F32 = jnp.float32
BF16 = jnp.bfloat16
I32 = jnp.int32
MESH = pl.DeviceIdType.MESH

SPRING = 5.0
C = 128
RAD = 64
NB = 8
SPECIES = 4
FAN = 16
HALO = 256
ATOMS = 1024
BLK = 256
BLOCKS = ATOMS // BLK
LANES = 128
WIN = LANES + 2 * HALO
TILES = ATOMS // LANES
TABLE = ATOMS + 2 * HALO
DEEP = (3, 7)
HID_UNROLL = 16
FAR_AWAY = 1.0e4


def lane_gather(source, index):
    return jnp.take_along_axis(source, index, axis=1, mode="promise_in_bounds")


def dot(a, b):
    return jnp.dot(a, b, preferred_element_type=F32)


def total(x):
    return jnp.sum(jnp.sum(x, axis=0, keepdims=True), axis=1, keepdims=True)


def one_hot_rows(local, iota):
    local = jnp.broadcast_to(local, (16, LANES)).astype(BF16)
    local = jnp.concatenate([local] * 16, axis=0)
    return jnp.where(local == iota, jnp.ones_like(iota), jnp.zeros_like(iota))


def side_by_side(left, right):
    return jnp.concatenate([left, right], axis=1)


def tile_of(lane):
    return slice(lane * LANES, (lane + 1) * LANES)


def kernel(
    n_img,
    n_atom,
    pos_in,
    species_in,
    counts_in,
    neighbours_in,
    send_list_in,
    climb,
    embed_in,
    ref_energy,
    rad_in_in,
    rad_out_in,
    mixing_in,
    w_energy_in,
    out,
    energy_out,
    pos,
    species,
    counts,
    neighbours,
    send_list,
    embed,
    rad_in,
    rad_out,
    mixing,
    w_energy,
    in_sem,
    ptab,
    sendpos,
    band,
    t1,
    t2,
    sendh,
    sendhot,
    iota_ref,
    hid,
    w_hid,
    w_first,
    rad_t,
    mix_t,
    emb_t,
    basis,
    sp_mask,
    delta,
    rel,
    scaled_ref,
    wide_ref,
    own_ref,
    force,
    tang,
    rbuf,
    pos_send,
    pos_recv,
    img_send,
    img_recv,
    h_send,
    h_recv,
    r_send,
    r_recv,
):
    img = lax.axis_index("img")
    me = lax.axis_index("atom")

    def ring(index, step, size):
        moved = index + step
        return jnp.where(moved >= size, moved - size, moved)

    up = ring(me, 1, n_atom)
    down = ring(me, n_atom - 1, n_atom)
    img_up = ring(img, 1, n_img)
    img_down = ring(img, n_img - 1, n_img)

    inputs = (
        (pos_in, pos),
        (species_in, species),
        (send_list_in, send_list),
        (embed_in, embed),
        (rad_in_in, rad_in),
        (rad_out_in, rad_out),
        (mixing_in, mixing),
        (neighbours_in, neighbours),
        (counts_in, counts),
        (w_energy_in, w_energy),
    )
    loads = [
        pltpu.make_async_copy(source, target, in_sem.at[n])
        for n, (source, target) in enumerate(inputs)
    ]
    for load in loads:
        load.start()
    low_last = lax.rem(me, n_atom // 2) == 0

    def low_turn(i):
        return jnp.logical_and(i >= 2, (i == 2) != low_last)

    def high_turn(i):
        return jnp.logical_and(i >= 2, (i == 2) == low_last)

    barrier = pltpu.get_barrier_semaphore()
    for d in range(1, n_atom):
        pl.semaphore_signal(
            barrier, inc=1, device_id=(img, ring(me, d, n_atom)), device_id_type=MESH
        )
    for other in (img_up, img_down):
        pl.semaphore_signal(barrier, inc=1, device_id=(other, me), device_id_type=MESH)

    for load in loads:
        load.wait()

    own_cols = slice(HALO, HALO + ATOMS)
    for comp in range(3):
        ptab[comp : comp + 1, own_cols] = pos[comp]
    ptab[3:4, own_cols] = species[...].astype(F32)
    ptab[4:8, own_cols] = jnp.zeros((4, ATOMS), F32)
    for t in range(4):
        index = jnp.broadcast_to(send_list[:, tile_of(t)], (8, LANES))
        low = index & 127
        high = index >> 7
        got = jnp.zeros((8, LANES), F32)
        for w in range(ATOMS // LANES):
            source = ptab[:, HALO + w * LANES : HALO + (w + 1) * LANES]
            got = jnp.where(high == w, lane_gather(source, low), got)
        sendpos[:, tile_of(t)] = got

    iota_ref[...] = lax.broadcasted_iota(I32, (256, LANES), 0).astype(F32).astype(BF16)
    for layer in range(3):
        rad_t[layer] = rad_out[layer].astype(F32).T.astype(BF16)
    for layer in range(2):
        mix_t[layer] = mixing[layer].astype(F32).T.astype(BF16)
    emb = embed[...].astype(F32)
    emb_rows = jnp.concatenate([emb, jnp.zeros((C - SPECIES, C), F32)], axis=0)
    emb_t[...] = emb_rows.T.astype(BF16)
    first = rad_out[0].astype(F32)
    w_first[...] = (
        jnp.concatenate([first * emb[k : k + 1, :] for k in range(SPECIES)], axis=0).T.astype(BF16)
    )
    lane = lax.broadcasted_iota(I32, (NB, C), 1)
    spread = (lane // FAN == lax.broadcasted_iota(I32, (NB, C), 0)).astype(F32).astype(BF16)
    lane64 = lax.broadcasted_iota(I32, (RAD, C), 1) % FAN
    for layer in range(3):
        wide = lax.dot_general(
            rad_in[layer], spread, (((0,), (0,)), ((), ())), preferred_element_type=F32
        )
        wide = wide * 0.5
        for s in range(FAN):
            start = s * 192 + layer * RAD
            w_hid[start : start + RAD, :] = jnp.where(lane64 == s, wide, 0.0).astype(BF16)

    def copy_to(source, target, send, recv, device):
        return pltpu.make_async_remote_copy(
            src_ref=source,
            dst_ref=target,
            send_sem=send,
            recv_sem=recv,
            device_id=device,
            device_id_type=MESH,
        )

    def pos_copies():
        low, high = slice(0, HALO), slice(HALO + ATOMS, TABLE)
        return (
            copy_to(
                sendpos.at[:, 0:HALO], ptab.at[:, high], pos_send.at[0], pos_recv.at[0], (img, down)
            ),
            copy_to(
                sendpos.at[:, HALO : 2 * HALO],
                ptab.at[:, low],
                pos_send.at[1],
                pos_recv.at[1],
                (img, up),
            ),
        )

    def img_copies():
        return (
            copy_to(pos, band.at[0], img_send.at[0], img_recv.at[0], (img_up, me)),
            copy_to(pos, band.at[1], img_send.at[1], img_recv.at[1], (img_down, me)),
        )

    def h_copies(phase, table):
        return (
            copy_to(
                sendh.at[phase, 0:2],
                table.at[10:12],
                h_send.at[phase, 0],
                h_recv.at[phase, 0],
                (img, down),
            ),
            copy_to(
                sendh.at[phase, 2:4],
                table.at[0:2],
                h_send.at[phase, 1],
                h_recv.at[phase, 1],
                (img, up),
            ),
        )

    lane_row = lax.broadcasted_iota(I32, (1, LANES), 1)

    def reduce_start(phase, values):
        message = jnp.zeros((1, LANES), F32)
        for n, value in enumerate(values):
            message = jnp.where(lane_row == n, value, message)
        rbuf[phase, me] = message
        for d in range(1, n_atom):
            copy_to(
                rbuf.at[phase, me],
                rbuf.at[phase, me],
                r_send.at[phase],
                r_recv.at[phase],
                (img, ring(me, d, n_atom)),
            ).start()

    def reduce_wait(phase, number):
        others = rbuf.at[phase, 0 : n_atom - 1]
        arrived = copy_to(others, others, r_send.at[phase], r_recv.at[phase], (img, up))
        arrived.wait_send()
        arrived.wait_recv()
        summed = jnp.sum(rbuf[phase], axis=0)
        return [
            jnp.sum(jnp.where(lane_row == n, summed, 0.0), axis=1, keepdims=True)
            for n in range(number)
        ]

    def radial(layer, tile, pair):
        sides = [
            hid[tile, pl.ds(pl.multiple_of((2 * pair + n) * 192 + layer * RAD, RAD), RAD), :]
            for n in range(2)
        ]
        return dot(rad_t[layer], side_by_side(*sides))

    def update_of(layer, t):
        half = dot(mix_t[layer], side_by_side(scaled_ref[t], scaled_ref[t + 1])) * 0.5
        return half + half * jnp.tanh(half)

    def first_sum(block, _):
        pieces = []
        for s in range(FAN):
            unit = side_by_side(
                *[hid[2 * block + t, s * 192 : s * 192 + RAD, :] for t in range(BLK // LANES)]
            )
            for k in range(SPECIES):
                mask = side_by_side(
                    *[
                        jnp.broadcast_to(sp_mask[2 * block + t, k, s : s + 1, :], (16, LANES))
                        for t in range(BLK // LANES)
                    ]
                ).astype(BF16)
                pieces.append(unit * jnp.concatenate([mask] * (RAD // 16), axis=0))
        wide = jnp.concatenate([w_first[...]] * FAN, axis=1)
        scaled = (dot(wide, jnp.concatenate(pieces, axis=0)) / math.sqrt(FAN)).astype(BF16)
        for t in range(BLK // LANES):
            scaled_ref[2 * block + t] = scaled[:, tile_of(t)]
        return 0

    def first_block(i, _):
        block = jnp.where(low_turn(i), 0, jnp.where(high_turn(i), BLOCKS - 1, i + 1))
        start = pl.multiple_of(block * BLK, BLK)

        @pl.when(i == 1)
        def _():
            pl.semaphore_wait(barrier, n_atom + 1)
            for copy in pos_copies() + img_copies():
                copy.start()

        @pl.when(i == 2)
        def _():
            for t in range(2 * HALO // LANES):
                index = send_list[:, tile_of(t)].astype(F32)
                for part in range(ATOMS // 256):
                    local = index - 256.0 * part
                    inside = jnp.logical_and(local >= 0.0, local < 256.0)
                    sendhot[t, part * 256 : (part + 1) * 256, :] = one_hot_rows(
                        jnp.where(inside, local, -1.0), iota_ref[...]
                    )

            lax.fori_loop(1, 3, first_sum, 0)

        @pl.when(low_turn(i))
        def _():
            pos_copies()[1].wait_recv()

        @pl.when(high_turn(i))
        def _():
            pos_copies()[0].wait_recv()

        @pl.when(i == 3)
        def _():
            for copy in pos_copies():
                copy.wait_send()
            for copy in img_copies():
                copy.wait()
            behind = pos[...] - band[0]
            ahead = band[1] - pos[...]
            reduce_start(
                0, (total(jnp.sum(behind * behind, axis=0)), total(jnp.sum(ahead * ahead, axis=0)))
            )

        for t in range(BLK // LANES):
            at = pl.multiple_of(start + t * LANES, LANES)
            tile = block * 2 + t
            offset = neighbours[:, pl.ds(at, LANES)] - at
            rel[tile] = offset
            low = offset & 127
            high = offset >> 7
            got = [None] * 4
            for w in range(WIN // LANES):
                here = high == w
                for comp in range(4):
                    source = jnp.broadcast_to(
                        ptab[comp : comp + 1, pl.ds(pl.multiple_of(at + w * LANES, LANES), LANES)],
                        (FAN, LANES),
                    )
                    value = lane_gather(source, low)
                    got[comp] = value if w == 0 else jnp.where(here, value, got[comp])
            slots = lax.broadcasted_iota(I32, (FAN, LANES), 0)
            live = slots < counts[:, pl.ds(at, LANES)]
            dist = jnp.zeros((FAN, LANES), F32)
            for comp in range(3):
                diff = got[comp] - pos[comp, :, pl.ds(at, LANES)]
                delta[comp, tile] = diff
                dist = dist + diff * diff
            dist = jnp.where(live, dist, FAR_AWAY)
            for k in range(NB):
                shifted = dist - 2.0 * k
                basis[t, k * FAN : (k + 1) * FAN, :] = jnp.exp(-(shifted * shifted) / 8.0).astype(
                    BF16
                )
            for k in range(SPECIES):
                sp_mask[tile, k] = (got[3] == float(k)).astype(F32)

        def slot(s, _):
            rows = pl.multiple_of(s * 192, 192)
            half = dot(w_hid[pl.ds(rows, 192), :], side_by_side(basis[0], basis[1]))
            unit = (half + half * jnp.tanh(half)).astype(BF16)
            for t in range(BLK // LANES):
                hid[block * 2 + t, pl.ds(rows, 192), :] = unit[:, tile_of(t)]
            return 0

        lax.fori_loop(0, FAN, slot, 0, unroll=HID_UNROLL)
        return 0

    lax.fori_loop(0, BLOCKS, first_block, 0)

    lax.fori_loop(3, 5, lambda i, _: first_sum(lax.rem(i, BLOCKS), 0), 0)
    for t in range(0, TILES, 2):
        kinds = jnp.broadcast_to(species[:, t * LANES : (t + 2) * LANES], (16, 2 * LANES))
        own_hot = (kinds == lax.broadcasted_iota(I32, kinds.shape, 0)).astype(F32).astype(BF16)
        h1 = (dot(emb_t[:, :16], own_hot) + update_of(0, t)).astype(BF16)
        for side in range(2):
            t1[t + side + 2] = h1[:, tile_of(side)]

    def lend(phase, table):
        own = jnp.concatenate([table[2 + t] for t in range(8)], axis=1)
        for side in range(2):
            lent = dot(own, side_by_side(sendhot[2 * side], sendhot[2 * side + 1])).astype(BF16)
            for t in range(2):
                sendh[phase, 2 * side + t] = lent[:, tile_of(t)]

    lend(0, t1)
    for copy in h_copies(0, t1):
        copy.start()

    def gathered(table, layer, tile, pair, nth):
        hot = side_by_side(
            *[
                one_hot_rows((rel[tile, 2 * pair + n : 2 * pair + n + 1, :] & 255).astype(F32), iota_ref[...])
                for n in range(2)
            ]
        )
        parts = 1 if pair in DEEP else 2
        near = jnp.concatenate(
            [side_by_side(table[tile + 2 * n], table[tile + 2 * n + 1]) for n in range(parts)],
            axis=0,
        )
        both = dot(near, hot)
        field = radial(layer + 1, tile, pair)
        far = []
        for side in range(2):
            index = jnp.broadcast_to(rel[tile, 2 * pair + side : 2 * pair + side + 1, :], (8, LANES))
            low = index & 127
            high = index >> 7
            pieces = []
            for g in range(C // 8):
                rows = slice(8 * g, 8 * g + 8)
                value = both[rows, tile_of(side)]
                if parts == 2:
                    later = both[C + 8 * g : C + 8 * g + 8, tile_of(side)]
                    value = jnp.where(high >= 2, later, value)
                else:
                    for n in range(2):
                        value = jnp.where(high == n + 2, lane_gather(wide_ref[nth + n, rows], low), value)
                pieces.append(jnp.where(high == 4, lane_gather(wide_ref[nth + 2, rows], low), value))
            far.append(jnp.concatenate(pieces, axis=0))
        return far, field

    def tile_loop(table, phase, body):
        def step(i, _):
            tile = jnp.where(low_turn(i), 0, jnp.where(high_turn(i), TILES - 2, 2 * i + 2))

            @pl.when(low_turn(i))
            def _():
                h_copies(phase, table)[1].wait_recv()

            @pl.when(high_turn(i))
            def _():
                h_copies(phase, table)[0].wait_recv()

            for n in range(4):
                wide_ref[n] = table[tile + 2 + n].astype(F32)
            for n in range(2):
                body(tile + n, n)
            return 0

        lax.fori_loop(0, TILES // 2, step, 0)
        for copy in h_copies(phase, table):
            copy.wait_send()

    def second_tile(tile, nth):
        summed = jnp.zeros((C, LANES), F32)
        for p in range(FAN // 2):
            far, field = gathered(t1, 0, tile, p, nth)
            summed = summed + (far[0] * field[:, tile_of(0)] + far[1] * field[:, tile_of(1)])
        scaled_ref[tile] = (summed / math.sqrt(FAN)).astype(BF16)

    tile_loop(t1, 0, second_tile)
    for t in range(0, TILES, 2):
        update = update_of(1, t)
        for side in range(2):
            at = t + side + 2
            t2[at] = (t1[at].astype(F32) + update[:, tile_of(side)]).astype(BF16)
    lend(1, t2)
    for copy in h_copies(1, t2):
        copy.start()
    back_sq, fore_sq = reduce_wait(0, 2)
    back_len = jnp.sqrt(back_sq + 1e-06)
    fore_len = jnp.sqrt(fore_sq + 1e-06)
    tangent = (pos[...] - band[0]) / back_len + (band[1] - pos[...]) / fore_len
    tang[...] = tangent
    reduce_start(1, (total(jnp.sum(tangent * tangent, axis=0)),))

    def force_tile(tile, nth):
        at = pl.multiple_of(tile * LANES, LANES)
        own_ref[nth] = t2[tile + 2].astype(F32)

        parts = [jnp.zeros((8, LANES), F32)] * 3
        for p in range(FAN // 2):
            far, field = gathered(t2, 1, tile, p, nth)
            for side in range(2):
                work = far[side] * field[:, tile_of(side)] * own_ref[nth]
                strip = jnp.sum(work.reshape(C // 8, 8, LANES), axis=0)
                row = 2 * p + side
                for comp in range(3):
                    parts[comp] = parts[comp] + strip * delta[comp, tile, row : row + 1, :]
        for comp in range(3):
            force[comp, :, pl.ds(at, LANES)] = jnp.sum(parts[comp], axis=0, keepdims=True) * (
                1.0 / math.sqrt(C)
            )

    tile_loop(t2, 1, force_tile)

    own = jnp.concatenate([t2[2 + t] for t in range(8)], axis=1)
    per_atom = dot(jnp.broadcast_to(w_energy[...], (16, C)), own)[0:1, :]
    for k in range(SPECIES):
        per_atom = per_atom + jnp.where(species[...] == k, ref_energy[k], 0.0)
    pull = force[...]
    tangent = tang[...]
    reduce_start(
        2,
        (
            jnp.sum(per_atom, axis=1, keepdims=True),
            total(jnp.sum(pull * tangent, axis=0)),
        ),
    )
    (tau_sq,) = reduce_wait(1, 1)
    energy, along = reduce_wait(2, 2)
    energy_out[...] = energy / (ATOMS * n_atom)
    proj = along / tau_sq
    interior = (
        pull - proj * tangent + SPRING * (fore_len - back_len) / jnp.sqrt(tau_sq) * tangent
    )
    climbing = pull - 2.0 * proj * tangent
    is_end = jnp.logical_or(img == 0, img == n_img - 1)
    band_force = jnp.where(climb[0] == 1, climbing, interior)
    out[...] = jnp.where(is_end, pull, band_force)


def finish(force, energy, force_out, energy_out):
    force_out[...] = force[...]
    energy_out[0] = energy[0, 0]


def on_device(
    n_img,
    n_atom,
    positions,
    species,
    counts,
    neighbours,
    send_list,
    climb,
    embed,
    ref_energy,
    rad_in,
    rad_out,
    mixing,
    w_energy,
):
    vmem = pl.BlockSpec(memory_space=pltpu.VMEM)
    smem = pl.BlockSpec(memory_space=pltpu.SMEM)
    hbm = pl.BlockSpec(memory_space=pltpu.HBM)
    dma = pltpu.SemaphoreType.DMA
    result, energy = pl.pallas_call(
        functools.partial(kernel, n_img, n_atom),
        out_shape=(
            jax.ShapeDtypeStruct((3, 1, ATOMS), F32),
            jax.ShapeDtypeStruct((1, 1), F32),
        ),
        in_specs=[hbm, hbm, hbm, hbm, hbm, smem, hbm, smem, hbm, hbm, hbm, hbm],
        out_specs=(vmem, vmem),
        scratch_shapes=[
            pltpu.VMEM((3, 1, ATOMS), F32),
            pltpu.VMEM((1, ATOMS), I32),
            pltpu.VMEM((1, ATOMS), I32),
            pltpu.VMEM((FAN, ATOMS), I32),
            pltpu.VMEM((1, 2 * HALO), I32),
            pltpu.VMEM(embed.shape, BF16),
            pltpu.VMEM(rad_in.shape, BF16),
            pltpu.VMEM(rad_out.shape, BF16),
            pltpu.VMEM(mixing.shape, BF16),
            pltpu.VMEM((1, C), BF16),
            dma((10,)),
            pltpu.VMEM((8, TABLE), F32),
            pltpu.VMEM((8, 2 * HALO), F32),
            pltpu.VMEM((2, 3, 1, ATOMS), F32),
            pltpu.VMEM((12, C, LANES), BF16),
            pltpu.VMEM((12, C, LANES), BF16),
            pltpu.VMEM((2, 4, C, LANES), BF16),
            pltpu.VMEM((4, ATOMS, LANES), BF16),
            pltpu.VMEM((256, LANES), BF16),
            pltpu.VMEM((TILES, FAN * 192, LANES), BF16),
            pltpu.VMEM((FAN * 192, C), BF16),
            pltpu.VMEM((C, 256), BF16),
            pltpu.VMEM((3, C, RAD), BF16),
            pltpu.VMEM((2, C, C), BF16),
            pltpu.VMEM((C, C), BF16),
            pltpu.VMEM((2, C, LANES), BF16),
            pltpu.VMEM((TILES, SPECIES, FAN, LANES), F32),
            pltpu.VMEM((3, TILES, FAN, LANES), F32),
            pltpu.VMEM((TILES, FAN, LANES), I32),
            pltpu.VMEM((TILES, C, LANES), BF16),
            pltpu.VMEM((4, C, LANES), F32),
            pltpu.VMEM((2, C, LANES), F32),
            pltpu.VMEM((3, 1, ATOMS), F32),
            pltpu.VMEM((3, 1, ATOMS), F32),
            pltpu.VMEM((3, n_atom, 1, LANES), F32),
            dma((2,)),
            dma((2,)),
            dma((2,)),
            dma((2,)),
            dma((2, 2)),
            dma((2, 2)),
            dma((3,)),
            dma((3,)),
        ],
        compiler_params=pltpu.CompilerParams(
            collective_id=0, has_side_effects=True, vmem_limit_bytes=60 * 1024 * 1024
        ),
        name="band_step",
    )(
        positions.transpose(1, 0, 2),
        species.reshape(1, ATOMS),
        counts.reshape(1, ATOMS),
        neighbours,
        send_list.reshape(1, 2 * HALO),
        climb,
        embed,
        ref_energy,
        rad_in,
        rad_out,
        mixing,
        w_energy.reshape(1, C),
    )
    result, energy = pl.pallas_call(
        finish,
        out_shape=(
            jax.ShapeDtypeStruct((3, 1, ATOMS), F32),
            jax.ShapeDtypeStruct((1,), F32),
        ),
        in_specs=[vmem, smem],
        out_specs=(vmem, smem),
        name="finish",
    )(result, energy)
    return result.transpose(1, 0, 2), energy


def solution(mesh):
    return jax.shard_map(
        functools.partial(on_device, mesh.shape["img"], mesh.shape["atom"]),
        mesh=mesh,
        in_specs=(
            P("img", None, "atom"),
            P("atom"),
            P("atom"),
            P(None, "atom"),
            P("atom"),
            P("img"),
            P(),
            P(),
            P(),
            P(),
            P(),
            P(),
        ),
        out_specs=(P("img", None, "atom"), P("img")),
        check_vma=False,
    )
```

```python
import functools
import math

import jax
import jax.numpy as jnp
from jax import lax
from jax.experimental import pallas as pl
from jax.experimental.pallas import tpu as pltpu
from jax.sharding import PartitionSpec as P

F32 = jnp.float32
BF16 = jnp.bfloat16
I32 = jnp.int32
MESH = pl.DeviceIdType.MESH

SPRING = 5.0
C = 128
RAD = 64
NB = 8
SPECIES = 4
FAN = 16
HALO = 256
ATOMS = 1024
BLK = 256
BLOCKS = ATOMS // BLK
LANES = 128
WIN = LANES + 2 * HALO
TILES = ATOMS // LANES
TABLE = ATOMS + 2 * HALO
DEEP = (3, 7)
HID_UNROLL = 16
FAR_AWAY = 1.0e4


def lane_gather(source, index):
    return jnp.take_along_axis(source, index, axis=1, mode="promise_in_bounds")


def dot(a, b):
    return jnp.dot(a, b, preferred_element_type=F32)


def total(x):
    return jnp.sum(jnp.sum(x, axis=0, keepdims=True), axis=1, keepdims=True)


def one_hot_rows(local, iota):
    local = jnp.broadcast_to(local, (16, LANES)).astype(BF16)
    local = jnp.concatenate([local] * 16, axis=0)
    return jnp.where(local == iota, jnp.ones_like(iota), jnp.zeros_like(iota))


def side_by_side(left, right):
    return jnp.concatenate([left, right], axis=1)


def far_first(n_atom):
    chips = n_atom // 4

    def hops(step):
        along = (step // 2) % chips
        return min(along, chips - along) + 2 * ((step // 2) // chips)

    return sorted(range(1, n_atom), key=lambda step: (-hops(step), step))


def tile_of(lane):
    return slice(lane * LANES, (lane + 1) * LANES)


def kernel(
    n_img,
    n_atom,
    pos_in,
    species_in,
    counts_in,
    neighbours_in,
    send_list_in,
    climb,
    embed_in,
    ref_energy,
    rad_in_in,
    rad_out_in,
    mixing_in,
    w_energy_in,
    out,
    energy_out,
    pos,
    species,
    counts,
    neighbours,
    send_list,
    embed,
    rad_in,
    rad_out,
    mixing,
    w_energy,
    in_sem,
    ptab,
    sendpos,
    band,
    t1,
    t2,
    sendh,
    sendhot,
    iota_ref,
    hid,
    w_hid,
    w_first,
    rad_t,
    mix_t,
    emb_t,
    basis,
    sp_mask,
    delta,
    rel,
    scaled_ref,
    wide_ref,
    own_ref,
    force,
    tang,
    rbuf,
    pos_send,
    pos_recv,
    img_send,
    img_recv,
    h_send,
    h_recv,
    r_send,
    r_recv,
):
    img = lax.axis_index("img")
    me = lax.axis_index("atom")

    def ring(index, step, size):
        moved = index + step
        return jnp.where(moved >= size, moved - size, moved)

    up = ring(me, 1, n_atom)
    down = ring(me, n_atom - 1, n_atom)
    img_up = ring(img, 1, n_img)
    img_down = ring(img, n_img - 1, n_img)

    inputs = (
        (pos_in, pos),
        (species_in, species),
        (send_list_in, send_list),
        (embed_in, embed),
        (rad_in_in, rad_in),
        (rad_out_in, rad_out),
        (mixing_in, mixing),
        (neighbours_in, neighbours),
        (counts_in, counts),
        (w_energy_in, w_energy),
    )
    loads = [
        pltpu.make_async_copy(source, target, in_sem.at[n])
        for n, (source, target) in enumerate(inputs)
    ]
    for load in loads:
        load.start()
    low_last = lax.rem(me, n_atom // 2) == 0

    def low_turn(i):
        return jnp.logical_and(i >= 2, (i == 2) != low_last)

    def high_turn(i):
        return jnp.logical_and(i >= 2, (i == 2) == low_last)

    barrier = pltpu.get_barrier_semaphore()
    for d in far_first(n_atom):
        pl.semaphore_signal(
            barrier, inc=1, device_id=(img, ring(me, d, n_atom)), device_id_type=MESH
        )
    for other in (img_up, img_down):
        pl.semaphore_signal(barrier, inc=1, device_id=(other, me), device_id_type=MESH)

    for load in loads[:3]:
        load.wait()

    own_cols = slice(HALO, HALO + ATOMS)
    for comp in range(3):
        ptab[comp : comp + 1, own_cols] = pos[comp]
    ptab[3:4, own_cols] = species[...].astype(F32)
    ptab[4:8, own_cols] = jnp.zeros((4, ATOMS), F32)
    for t in range(4):
        index = jnp.broadcast_to(send_list[:, tile_of(t)], (8, LANES))
        low = index & 127
        high = index >> 7
        got = jnp.zeros((8, LANES), F32)
        for w in range(ATOMS // LANES):
            source = ptab[:, HALO + w * LANES : HALO + (w + 1) * LANES]
            got = jnp.where(high == w, lane_gather(source, low), got)
        sendpos[:, tile_of(t)] = got

    for load in loads[3:7]:
        load.wait()

    iota_ref[...] = lax.broadcasted_iota(I32, (256, LANES), 0).astype(F32).astype(BF16)
    for layer in range(3):
        rad_t[layer] = rad_out[layer].astype(F32).T.astype(BF16)
    for layer in range(2):
        mix_t[layer] = mixing[layer].astype(F32).T.astype(BF16)
    emb = embed[...].astype(F32)
    emb_rows = jnp.concatenate([emb, jnp.zeros((C - SPECIES, C), F32)], axis=0)
    emb_t[...] = emb_rows.T.astype(BF16)
    first = rad_out[0].astype(F32)
    w_first[...] = (
        jnp.concatenate([first * emb[k : k + 1, :] for k in range(SPECIES)], axis=0).T.astype(BF16)
    )
    lane = lax.broadcasted_iota(I32, (NB, C), 1)
    spread = (lane // FAN == lax.broadcasted_iota(I32, (NB, C), 0)).astype(F32).astype(BF16)
    lane64 = lax.broadcasted_iota(I32, (RAD, C), 1) % FAN
    for layer in range(3):
        wide = lax.dot_general(
            rad_in[layer], spread, (((0,), (0,)), ((), ())), preferred_element_type=F32
        )
        wide = wide * 0.5
        for s in range(FAN):
            start = s * 192 + layer * RAD
            w_hid[start : start + RAD, :] = jnp.where(lane64 == s, wide, 0.0).astype(BF16)

    for load in loads[7:]:
        load.wait()

    def copy_to(source, target, send, recv, device):
        return pltpu.make_async_remote_copy(
            src_ref=source,
            dst_ref=target,
            send_sem=send,
            recv_sem=recv,
            device_id=device,
            device_id_type=MESH,
        )

    def pos_copies():
        low, high = slice(0, HALO), slice(HALO + ATOMS, TABLE)
        return (
            copy_to(
                sendpos.at[:, 0:HALO], ptab.at[:, high], pos_send.at[0], pos_recv.at[0], (img, down)
            ),
            copy_to(
                sendpos.at[:, HALO : 2 * HALO],
                ptab.at[:, low],
                pos_send.at[1],
                pos_recv.at[1],
                (img, up),
            ),
        )

    def img_copies():
        return (
            copy_to(pos, band.at[0], img_send.at[0], img_recv.at[0], (img_up, me)),
            copy_to(pos, band.at[1], img_send.at[1], img_recv.at[1], (img_down, me)),
        )

    def h_copies(phase, table):
        return (
            copy_to(
                sendh.at[phase, 0:2],
                table.at[10:12],
                h_send.at[phase, 0],
                h_recv.at[phase, 0],
                (img, down),
            ),
            copy_to(
                sendh.at[phase, 2:4],
                table.at[0:2],
                h_send.at[phase, 1],
                h_recv.at[phase, 1],
                (img, up),
            ),
        )

    lane_row = lax.broadcasted_iota(I32, (1, LANES), 1)

    def reduce_start(phase, values):
        message = jnp.zeros((1, LANES), F32)
        for n, value in enumerate(values):
            message = jnp.where(lane_row == n, value, message)
        rbuf[phase, me] = message
        for d in far_first(n_atom):
            copy_to(
                rbuf.at[phase, me],
                rbuf.at[phase, me],
                r_send.at[phase],
                r_recv.at[phase],
                (img, ring(me, d, n_atom)),
            ).start()

    def reduce_wait(phase, number):
        others = rbuf.at[phase, 0 : n_atom - 1]
        arrived = copy_to(others, others, r_send.at[phase], r_recv.at[phase], (img, up))
        arrived.wait_send()
        arrived.wait_recv()
        summed = jnp.sum(rbuf[phase], axis=0)
        return [
            jnp.sum(jnp.where(lane_row == n, summed, 0.0), axis=1, keepdims=True)
            for n in range(number)
        ]

    def radial(layer, tile, pair):
        sides = [
            hid[tile, pl.ds(pl.multiple_of((2 * pair + n) * 192 + layer * RAD, RAD), RAD), :]
            for n in range(2)
        ]
        return dot(rad_t[layer], side_by_side(*sides))

    def update_of(layer, t):
        half = dot(mix_t[layer], side_by_side(scaled_ref[t], scaled_ref[t + 1])) * 0.5
        return half + half * jnp.tanh(half)

    def first_sum(block, _):
        pieces = []
        for s in range(FAN):
            unit = side_by_side(
                *[hid[2 * block + t, s * 192 : s * 192 + RAD, :] for t in range(BLK // LANES)]
            )
            for k in range(SPECIES):
                mask = side_by_side(
                    *[
                        jnp.broadcast_to(sp_mask[2 * block + t, k, s : s + 1, :], (16, LANES))
                        for t in range(BLK // LANES)
                    ]
                ).astype(BF16)
                pieces.append(unit * jnp.concatenate([mask] * (RAD // 16), axis=0))
        wide = jnp.concatenate([w_first[...]] * FAN, axis=1)
        scaled = (dot(wide, jnp.concatenate(pieces, axis=0)) / math.sqrt(FAN)).astype(BF16)
        for t in range(BLK // LANES):
            scaled_ref[2 * block + t] = scaled[:, tile_of(t)]
        return 0

    def first_block(i, _):
        block = jnp.where(low_turn(i), 0, jnp.where(high_turn(i), BLOCKS - 1, i + 1))
        start = pl.multiple_of(block * BLK, BLK)

        @pl.when(i == 1)
        def _():
            pl.semaphore_wait(barrier, n_atom + 1)
            for copy in pos_copies() + img_copies():
                copy.start()

        @pl.when(i == 2)
        def _():
            for t in range(2 * HALO // LANES):
                index = send_list[:, tile_of(t)].astype(F32)
                for part in range(ATOMS // 256):
                    local = index - 256.0 * part
                    inside = jnp.logical_and(local >= 0.0, local < 256.0)
                    sendhot[t, part * 256 : (part + 1) * 256, :] = one_hot_rows(
                        jnp.where(inside, local, -1.0), iota_ref[...]
                    )

            lax.fori_loop(1, 3, first_sum, 0)

        @pl.when(low_turn(i))
        def _():
            pos_copies()[1].wait_recv()

        @pl.when(high_turn(i))
        def _():
            pos_copies()[0].wait_recv()

        @pl.when(i == 3)
        def _():
            for copy in pos_copies():
                copy.wait_send()
            for copy in img_copies():
                copy.wait()
            behind = pos[...] - band[0]
            ahead = band[1] - pos[...]
            reduce_start(
                0, (total(jnp.sum(behind * behind, axis=0)), total(jnp.sum(ahead * ahead, axis=0)))
            )

        for t in range(BLK // LANES):
            at = pl.multiple_of(start + t * LANES, LANES)
            tile = block * 2 + t
            offset = neighbours[:, pl.ds(at, LANES)] - at
            rel[tile] = offset
            low = offset & 127
            high = offset >> 7
            got = [None] * 4
            for w in range(WIN // LANES):
                here = high == w
                for comp in range(4):
                    source = jnp.broadcast_to(
                        ptab[comp : comp + 1, pl.ds(pl.multiple_of(at + w * LANES, LANES), LANES)],
                        (FAN, LANES),
                    )
                    value = lane_gather(source, low)
                    got[comp] = value if w == 0 else jnp.where(here, value, got[comp])
            slots = lax.broadcasted_iota(I32, (FAN, LANES), 0)
            live = slots < counts[:, pl.ds(at, LANES)]
            dist = jnp.zeros((FAN, LANES), F32)
            for comp in range(3):
                diff = got[comp] - pos[comp, :, pl.ds(at, LANES)]
                delta[comp, tile] = diff
                dist = dist + diff * diff
            dist = jnp.where(live, dist, FAR_AWAY)
            for k in range(NB):
                shifted = dist - 2.0 * k
                basis[t, k * FAN : (k + 1) * FAN, :] = jnp.exp(-(shifted * shifted) / 8.0).astype(
                    BF16
                )
            for k in range(SPECIES):
                sp_mask[tile, k] = (got[3] == float(k)).astype(F32)

        def slot(s, _):
            rows = pl.multiple_of(s * 192, 192)
            half = dot(w_hid[pl.ds(rows, 192), :], side_by_side(basis[0], basis[1]))
            unit = (half + half * jnp.tanh(half)).astype(BF16)
            for t in range(BLK // LANES):
                hid[block * 2 + t, pl.ds(rows, 192), :] = unit[:, tile_of(t)]
            return 0

        lax.fori_loop(0, FAN, slot, 0, unroll=HID_UNROLL)
        return 0

    lax.fori_loop(0, BLOCKS, first_block, 0)

    lax.fori_loop(3, 5, lambda i, _: first_sum(lax.rem(i, BLOCKS), 0), 0)
    for t in range(0, TILES, 2):
        kinds = jnp.broadcast_to(species[:, t * LANES : (t + 2) * LANES], (16, 2 * LANES))
        own_hot = (kinds == lax.broadcasted_iota(I32, kinds.shape, 0)).astype(F32).astype(BF16)
        h1 = (dot(emb_t[:, :16], own_hot) + update_of(0, t)).astype(BF16)
        for side in range(2):
            t1[t + side + 2] = h1[:, tile_of(side)]

    def lend(phase, table):
        own = jnp.concatenate([table[2 + t] for t in range(8)], axis=1)
        for side in range(2):
            lent = dot(own, side_by_side(sendhot[2 * side], sendhot[2 * side + 1])).astype(BF16)
            for t in range(2):
                sendh[phase, 2 * side + t] = lent[:, tile_of(t)]

    lend(0, t1)
    for copy in h_copies(0, t1):
        copy.start()

    def gathered(table, layer, tile, pair, nth):
        hot = side_by_side(
            *[
                one_hot_rows((rel[tile, 2 * pair + n : 2 * pair + n + 1, :] & 255).astype(F32), iota_ref[...])
                for n in range(2)
            ]
        )
        parts = 1 if pair in DEEP else 2
        near = jnp.concatenate(
            [side_by_side(table[tile + 2 * n], table[tile + 2 * n + 1]) for n in range(parts)],
            axis=0,
        )
        both = dot(near, hot)
        field = radial(layer + 1, tile, pair)
        far = []
        for side in range(2):
            index = jnp.broadcast_to(rel[tile, 2 * pair + side : 2 * pair + side + 1, :], (8, LANES))
            low = index & 127
            high = index >> 7
            pieces = []
            for g in range(C // 8):
                rows = slice(8 * g, 8 * g + 8)
                value = both[rows, tile_of(side)]
                if parts == 2:
                    later = both[C + 8 * g : C + 8 * g + 8, tile_of(side)]
                    value = jnp.where(high >= 2, later, value)
                else:
                    for n in range(2):
                        value = jnp.where(high == n + 2, lane_gather(wide_ref[nth + n, rows], low), value)
                pieces.append(jnp.where(high == 4, lane_gather(wide_ref[nth + 2, rows], low), value))
            far.append(jnp.concatenate(pieces, axis=0))
        return far, field

    def tile_loop(table, phase, body):
        def step(i, _):
            tile = jnp.where(low_turn(i), 0, jnp.where(high_turn(i), TILES - 2, 2 * i + 2))

            @pl.when(low_turn(i))
            def _():
                h_copies(phase, table)[1].wait_recv()

            @pl.when(high_turn(i))
            def _():
                h_copies(phase, table)[0].wait_recv()

            for n in range(4):
                wide_ref[n] = table[tile + 2 + n].astype(F32)
            for n in range(2):
                body(tile + n, n)
            return 0

        lax.fori_loop(0, TILES // 2, step, 0)
        for copy in h_copies(phase, table):
            copy.wait_send()

    def second_tile(tile, nth):
        summed = jnp.zeros((C, LANES), F32)
        for p in range(FAN // 2):
            far, field = gathered(t1, 0, tile, p, nth)
            summed = summed + (far[0] * field[:, tile_of(0)] + far[1] * field[:, tile_of(1)])
        scaled_ref[tile] = (summed / math.sqrt(FAN)).astype(BF16)

    tile_loop(t1, 0, second_tile)
    for t in range(0, TILES, 2):
        update = update_of(1, t)
        for side in range(2):
            at = t + side + 2
            t2[at] = (t1[at].astype(F32) + update[:, tile_of(side)]).astype(BF16)
    lend(1, t2)
    for copy in h_copies(1, t2):
        copy.start()
    back_sq, fore_sq = reduce_wait(0, 2)
    back_len = jnp.sqrt(back_sq + 1e-06)
    fore_len = jnp.sqrt(fore_sq + 1e-06)
    tangent = (pos[...] - band[0]) / back_len + (band[1] - pos[...]) / fore_len
    tang[...] = tangent
    reduce_start(1, (total(jnp.sum(tangent * tangent, axis=0)),))

    def force_tile(tile, nth):
        at = pl.multiple_of(tile * LANES, LANES)
        own_ref[nth] = t2[tile + 2].astype(F32)

        parts = [jnp.zeros((8, LANES), F32)] * 3
        for p in range(FAN // 2):
            far, field = gathered(t2, 1, tile, p, nth)
            for side in range(2):
                work = far[side] * field[:, tile_of(side)] * own_ref[nth]
                strip = jnp.sum(work.reshape(C // 8, 8, LANES), axis=0)
                row = 2 * p + side
                for comp in range(3):
                    parts[comp] = parts[comp] + strip * delta[comp, tile, row : row + 1, :]
        for comp in range(3):
            force[comp, :, pl.ds(at, LANES)] = jnp.sum(parts[comp], axis=0, keepdims=True) * (
                1.0 / math.sqrt(C)
            )

    tile_loop(t2, 1, force_tile)

    own = jnp.concatenate([t2[2 + t] for t in range(8)], axis=1)
    per_atom = dot(jnp.broadcast_to(w_energy[...], (16, C)), own)[0:1, :]
    for k in range(SPECIES):
        per_atom = per_atom + jnp.where(species[...] == k, ref_energy[k], 0.0)
    pull = force[...]
    tangent = tang[...]
    reduce_start(
        2,
        (
            jnp.sum(per_atom, axis=1, keepdims=True),
            total(jnp.sum(pull * tangent, axis=0)),
        ),
    )
    (tau_sq,) = reduce_wait(1, 1)
    energy, along = reduce_wait(2, 2)
    energy_out[...] = energy / (ATOMS * n_atom)
    proj = along / tau_sq
    interior = (
        pull - proj * tangent + SPRING * (fore_len - back_len) / jnp.sqrt(tau_sq) * tangent
    )
    climbing = pull - 2.0 * proj * tangent
    is_end = jnp.logical_or(img == 0, img == n_img - 1)
    band_force = jnp.where(climb[0] == 1, climbing, interior)
    out[...] = jnp.where(is_end, pull, band_force)


def finish(force, energy, force_out, energy_out):
    force_out[...] = force[...]
    energy_out[0] = energy[0, 0]


def on_device(
    n_img,
    n_atom,
    positions,
    species,
    counts,
    neighbours,
    send_list,
    climb,
    embed,
    ref_energy,
    rad_in,
    rad_out,
    mixing,
    w_energy,
):
    vmem = pl.BlockSpec(memory_space=pltpu.VMEM)
    smem = pl.BlockSpec(memory_space=pltpu.SMEM)
    hbm = pl.BlockSpec(memory_space=pltpu.HBM)
    dma = pltpu.SemaphoreType.DMA
    result, energy = pl.pallas_call(
        functools.partial(kernel, n_img, n_atom),
        out_shape=(
            jax.ShapeDtypeStruct((3, 1, ATOMS), F32),
            jax.ShapeDtypeStruct((1, 1), F32),
        ),
        in_specs=[hbm, hbm, hbm, hbm, hbm, smem, hbm, smem, hbm, hbm, hbm, hbm],
        out_specs=(vmem, vmem),
        scratch_shapes=[
            pltpu.VMEM((3, 1, ATOMS), F32),
            pltpu.VMEM((1, ATOMS), I32),
            pltpu.VMEM((1, ATOMS), I32),
            pltpu.VMEM((FAN, ATOMS), I32),
            pltpu.VMEM((1, 2 * HALO), I32),
            pltpu.VMEM(embed.shape, BF16),
            pltpu.VMEM(rad_in.shape, BF16),
            pltpu.VMEM(rad_out.shape, BF16),
            pltpu.VMEM(mixing.shape, BF16),
            pltpu.VMEM((1, C), BF16),
            dma((10,)),
            pltpu.VMEM((8, TABLE), F32),
            pltpu.VMEM((8, 2 * HALO), F32),
            pltpu.VMEM((2, 3, 1, ATOMS), F32),
            pltpu.VMEM((12, C, LANES), BF16),
            pltpu.VMEM((12, C, LANES), BF16),
            pltpu.VMEM((2, 4, C, LANES), BF16),
            pltpu.VMEM((4, ATOMS, LANES), BF16),
            pltpu.VMEM((256, LANES), BF16),
            pltpu.VMEM((TILES, FAN * 192, LANES), BF16),
            pltpu.VMEM((FAN * 192, C), BF16),
            pltpu.VMEM((C, 256), BF16),
            pltpu.VMEM((3, C, RAD), BF16),
            pltpu.VMEM((2, C, C), BF16),
            pltpu.VMEM((C, C), BF16),
            pltpu.VMEM((2, C, LANES), BF16),
            pltpu.VMEM((TILES, SPECIES, FAN, LANES), F32),
            pltpu.VMEM((3, TILES, FAN, LANES), F32),
            pltpu.VMEM((TILES, FAN, LANES), I32),
            pltpu.VMEM((TILES, C, LANES), BF16),
            pltpu.VMEM((4, C, LANES), F32),
            pltpu.VMEM((2, C, LANES), F32),
            pltpu.VMEM((3, 1, ATOMS), F32),
            pltpu.VMEM((3, 1, ATOMS), F32),
            pltpu.VMEM((3, n_atom, 1, LANES), F32),
            dma((2,)),
            dma((2,)),
            dma((2,)),
            dma((2,)),
            dma((2, 2)),
            dma((2, 2)),
            dma((3,)),
            dma((3,)),
        ],
        compiler_params=pltpu.CompilerParams(
            collective_id=0, has_side_effects=True, vmem_limit_bytes=60 * 1024 * 1024
        ),
        name="band_step",
    )(
        positions.transpose(1, 0, 2),
        species.reshape(1, ATOMS),
        counts.reshape(1, ATOMS),
        neighbours,
        send_list.reshape(1, 2 * HALO),
        climb,
        embed,
        ref_energy,
        rad_in,
        rad_out,
        mixing,
        w_energy.reshape(1, C),
    )
    result, energy = pl.pallas_call(
        finish,
        out_shape=(
            jax.ShapeDtypeStruct((3, 1, ATOMS), F32),
            jax.ShapeDtypeStruct((1,), F32),
        ),
        in_specs=[vmem, smem],
        out_specs=(vmem, smem),
        name="finish",
    )(result, energy)
    return result.transpose(1, 0, 2), energy


def solution(mesh):
    return jax.shard_map(
        functools.partial(on_device, mesh.shape["img"], mesh.shape["atom"]),
        mesh=mesh,
        in_specs=(
            P("img", None, "atom"),
            P("atom"),
            P("atom"),
            P(None, "atom"),
            P("atom"),
            P("img"),
            P(),
            P(),
            P(),
            P(),
            P(),
            P(),
        ),
        out_specs=(P("img", None, "atom"), P("img")),
        check_vma=False,
    )
```
